512 devices in a mesh: ep: 64 (over z, y), dp: 8 (over x, core).
Axes of the slice: x: 4, y: 4, z: 16, core: 2. Of those that a mesh axis runs over, the one named last changes fastest.
Arguments:
- tokens: bfloat16 [12288, 3584], P(('ep', 'dp')), may hold values from -6 to 6
- grad_out: bfloat16 [12288, 3584], P(('ep', 'dp')), may hold values from -0.29882812 to 0.29882812
- routes: int32 [12288, 2], P(('ep', 'dp')), may hold values from 0 to 7, all different within a row; in each aligned block of 24 rows (0 to 23, 24 to 47, ...) at most 8 rows name the same one
- route_probs: float32 [12288, 2], P(('ep', 'dp')), may hold values from 0.1 to 1
- gate_weight: bfloat16 [64, 3584, 128], P('ep', 'dp'), may hold values from -0.09375 to 0.09375
- up_weight: bfloat16 [64, 3584, 128], P('ep', 'dp'), may hold values from -0.09375 to 0.09375
- down_weight: bfloat16 [64, 3584, 128], P('ep', 'dp'), may hold values from -0.1875 to 0.1875
Outputs:
- grad_tokens: bfloat16 [12288, 3584], P(('ep', 'dp'))
- grad_probs: float32 [12288, 2], P(('ep', 'dp'))
- grad_gate: bfloat16 [64, 3584, 128], P('ep', 'dp')
- grad_up: bfloat16 [64, 3584, 128], P('ep', 'dp')
- grad_down: bfloat16 [64, 3584, 128], P('ep', 'dp')
The draws below stay inside these ranges and needn't reach their ends.
Inputs may be any that keep to these rules, and one draw needn't show every extreme that they name: `routes`: each row names 2 different experts. Within each aligned block of 24 rows (the tokens of one device) no expert is named by more than 8 rows; in some blocks one expert is named by exactly 8 rows.
All inputs are finite; a program needn't handle non-finite values.
Results may differ from the reference program's by a relative error of at most 0.017.
Values may be sent and summed in bfloat16 or wider, within the bound.
No kernel may reach another device: no remote copies, remote signals or barrier semaphores. Data moves between devices by JAX's collectives and lax.ppermute only.
A program may use at most 64 MiB of HBM per device.

```python
import math
import jax
import jax.numpy as jnp
import numpy as np
from jax import lax

D = 3584
HIDDEN_SIZE = 1024
GROUP = 8
TOP = 2
TOK_DEV = 24
EXPERTS = 8
HID_DEV = 128
SLICES = 64
CAP = 8
TOKENS = 12288
N_EP = 64
N_DP = 8


def shard_levels(stream_key, dims, shards, low, largest):
    loudness, own = 1.0, jax.random.fold_in(stream_key, 6)
    for position, parts in shards:
        draws = jnp.exp(jax.random.uniform(jax.random.fold_in(own, position), (parts,), jnp.float32, low / len(shards), largest / len(shards)))
        loudness = loudness * jnp.repeat(draws, dims[position] // parts).reshape([-1 if axis == position else 1 for axis in range(len(dims))])
    return loudness


def routed_block(rng, own, number, rows, number_of, top, reach, lean):
    sequence = jax.random.permutation(rng, number_of)
    heavy_load, usual = shares(number_of, rows * top, reach, lean, True), shares(number_of, rows * top, reach, lean, False)
    places = jnp.arange(number_of)

    def named(lengths, rotation):
        used = int((lengths > 0).sum())
        fixed = max(1, used // 4)
        moved = fixed + (places - fixed + rotation * (used - fixed)) % max(1, number_of - fixed)
        return jnp.zeros((number_of,), jnp.int32).at[sequence[jnp.where(places < fixed, places, moved)]].set(jnp.asarray(lengths, jnp.int32))

    lengths = jnp.where(number % 4 == 0, named(heavy_load, number // 4), named(usual, number - number // 4 - 1))
    mixed = jax.random.permutation(jax.random.fold_in(own, 3), number_of)
    source_of, receiver = mixed[0:number_of // 2 * 2:2], mixed[1:number_of // 2 * 2:2]
    room = jnp.minimum(lengths[source_of] - 1, reach - lengths[receiver]) // 2
    room = jnp.where((source_of == sequence[0]) | (receiver == sequence[0]) | (lengths[receiver] == 0), 0, jnp.maximum(room, 0))
    moved = jax.random.randint(jax.random.fold_in(own, 4), (number_of // 2,), 0, 1 << 20) % (room + 1)
    lengths = lengths.at[source_of].add(-moved).at[receiver].add(moved)
    members = jnp.searchsorted(jnp.cumsum(lengths), jnp.arange(rows * top), side="right").astype(jnp.int32)
    grid = members.reshape(top, rows).T
    grid = grid[jax.random.permutation(jax.random.fold_in(own, 1), rows)]
    rotation = jax.random.randint(jax.random.fold_in(own, 2), (rows, 1), 0, top)
    return jnp.take_along_axis(grid, (jnp.arange(top)[None, :] + rotation) % top, axis=1)


def shares(count, total, limit, slope, full):
    weights = [(1 << 20) // math.isqrt(grade ** slope) + 1 for grade in range(1, count + 1)]
    largest = limit if full else min(limit, max(-(-total // count), total * weights[0] // sum(weights)))
    least = 1 if total - largest >= count - 1 else 0
    holding, surplus = [largest] + [least] * (count - 1), total - largest - least * (count - 1)
    while surplus > 0:
        free = [i for i in range(1, count) if holding[i] < largest] or [i for i in range(1, count) if holding[i] < limit]
        mass, left = sum([weights[i] for i in free]), surplus
        for i in free:
            addition = min(limit - holding[i], max(1, left * weights[i] // mass), surplus)
            holding[i] = holding[i] + addition
            surplus = surplus - addition
    return np.array(holding)


def noise(key, shape, spread, limit, cuts=(), kind=jnp.bfloat16):
    entries = jax.random.normal(key, shape, jnp.float32) * spread
    if len(cuts) > 0:
        entries = shard_levels(key, shape, cuts, -0.22, 0.18) * entries
    return jnp.clip(entries, min=-limit, max=limit).astype(kind)


def setup_inputs(seed: int = 0) -> dict:
    streams_of = jax.random.split(jax.random.key(seed), 8)
    tokens = noise(streams_of[0], (TOKENS, D), 1.0, 6.0, ((0, 512),))
    grad_out = noise(streams_of[1], (TOKENS, D), 0.05, 0.29882812, ((0, 512),))
    routes_keys = jax.random.split(jax.random.fold_in(streams_of[2], 1), TOKENS // TOK_DEV)
    routes_turns = jax.random.permutation(jax.random.fold_in(streams_of[2], 3), TOKENS // TOK_DEV)
    routes = jax.vmap(lambda own, number: routed_block(jax.random.fold_in(streams_of[2], 2), own, number, TOK_DEV, EXPERTS, TOP, CAP, 2))(routes_keys, routes_turns).reshape((TOKENS, TOP))
    route_probs = jnp.clip(0.1 + 0.9 * jax.random.uniform(streams_of[3], (TOKENS, TOP), jnp.float32) ** shard_levels(streams_of[3], (TOKENS, TOP), ((0, 512),), -0.2, 0.2), 0.1, 1.0)
    gate_weight = noise(streams_of[4], (SLICES, D, HID_DEV), D ** -0.5, 0.09375, ((0, 64), (1, 8)))
    up_weight = noise(streams_of[5], (SLICES, D, HID_DEV), D ** -0.5, 0.09375, ((0, 64), (1, 8)))
    down_weight = noise(streams_of[6], (SLICES, D, HID_DEV), HIDDEN_SIZE ** -0.5, 0.1875, ((0, 64), (1, 8)))
    return {"tokens": tokens, "grad_out": grad_out, "routes": routes, "route_probs": route_probs, "gate_weight": gate_weight, "up_weight": up_weight, "down_weight": down_weight}


CONTRACT_HIDDEN = (((1,), (1,)), ((), ()))
CONTRACT_ROWS = (((0,), (0,)), ((), ()))


def slot_table(routes):
    copies = TOKENS * TOP
    blocks = N_EP * N_DP
    block_routes = routes.reshape(blocks, TOK_DEV * TOP)
    onehot = (block_routes[:, :, None] == jnp.arange(EXPERTS, dtype=jnp.int32)[None, None, :]).astype(jnp.int32)
    earlier = jnp.cumsum(onehot, axis=1) - onehot
    slot_rank = jnp.sum(earlier * onehot, axis=2)
    block_ids = jnp.arange(blocks, dtype=jnp.int32)[:, None] * jnp.ones((1, TOK_DEV * TOP), jnp.int32)
    row_place = (block_ids // N_DP) * CAP + slot_rank
    group_place = block_ids % N_DP
    table = jnp.full((EXPERTS, N_DP, N_EP * CAP), copies, jnp.int32)
    return table.at[block_routes.reshape(-1), group_place.reshape(-1), row_place.reshape(-1)].set(
        jnp.arange(copies, dtype=jnp.int32))


def expert_full(weight, expert):
    blocks_of = lax.dynamic_slice_in_dim(weight, (expert * GROUP).astype(jnp.int32), GROUP, 0)
    return jnp.transpose(blocks_of, (1, 0, 2)).reshape(D, HIDDEN_SIZE)


def reference(tokens, grad_out, routes, route_probs, gate_weight, up_weight, down_weight):
    copies = TOKENS * TOP
    table = slot_table(routes)
    flat_probs = route_probs.reshape(-1)

    def expert_step(carry, expert):
        gate_full = expert_full(gate_weight, expert)
        up_full = expert_full(up_weight, expert)
        down_full = expert_full(down_weight, expert)
        gate_split = gate_full.astype(jnp.float32).reshape(D, GROUP, HID_DEV)
        up_split = up_full.astype(jnp.float32).reshape(D, GROUP, HID_DEV)

        def group_step(inner, group_index):
            token_acc, score_acc, grad_acc = inner
            copy_ids = table[expert, group_index]
            valid = copy_ids < copies
            safe_ids = jnp.where(valid, copy_ids, 0)
            token_ids = safe_ids // TOP
            rows_in = jnp.where(valid[:, None], tokens[token_ids], jnp.zeros((), tokens.dtype))
            rows_grad = jnp.where(valid[:, None], grad_out[token_ids], jnp.zeros((), grad_out.dtype))
            rows_prob = jnp.where(valid, flat_probs[safe_ids], jnp.zeros((), flat_probs.dtype))
            gate_pre = jnp.dot(rows_in, gate_full, preferred_element_type=jnp.float32)
            up_pre = jnp.dot(rows_in, up_full, preferred_element_type=jnp.float32)
            sigmoid_gate = jax.nn.sigmoid(gate_pre)
            activated = gate_pre * sigmoid_gate
            hidden = (activated * up_pre).astype(jnp.bfloat16)
            scaled = (rows_prob[:, None] * rows_grad.astype(jnp.float32)).astype(jnp.bfloat16)
            down_grad = jnp.dot(rows_grad, down_full, preferred_element_type=jnp.float32)
            scores = jnp.sum(hidden.astype(jnp.float32) * down_grad, axis=1)
            hidden_grad = rows_prob[:, None] * down_grad
            gate_grad = (hidden_grad * up_pre * sigmoid_gate * (1.0 + gate_pre * (1.0 - sigmoid_gate))).astype(jnp.bfloat16)
            up_grad = (hidden_grad * activated).astype(jnp.bfloat16)
            slice_terms = jnp.einsum("rgh,dgh->rgd", gate_grad.astype(jnp.float32).reshape(-1, GROUP, HID_DEV), gate_split)
            slice_terms = slice_terms + jnp.einsum("rgh,dgh->rgd", up_grad.astype(jnp.float32).reshape(-1, GROUP, HID_DEV), up_split)
            rounded = lax.optimization_barrier(slice_terms.astype(jnp.bfloat16))
            token_rows = jnp.sum(rounded.astype(jnp.float32), axis=1)
            token_acc = token_acc.at[token_ids].add(jnp.where(valid[:, None], token_rows, 0.0))
            score_acc = score_acc.at[safe_ids].add(jnp.where(valid, scores, 0.0))
            gate_term = lax.dot_general(rows_in, gate_grad, CONTRACT_ROWS, preferred_element_type=jnp.float32)
            up_term = lax.dot_general(rows_in, up_grad, CONTRACT_ROWS, preferred_element_type=jnp.float32)
            down_term = lax.dot_general(scaled, hidden, CONTRACT_ROWS, preferred_element_type=jnp.float32)
            terms = lax.optimization_barrier(jnp.stack([gate_term, up_term, down_term]).astype(jnp.bfloat16))
            return (token_acc, score_acc, grad_acc + terms.astype(jnp.float32)), None

        token_acc, score_acc = carry
        start_grads = jnp.zeros((3, D, HIDDEN_SIZE), jnp.float32)
        (token_acc, score_acc, grad_acc), _ = lax.scan(
            group_step, (token_acc, score_acc, start_grads), jnp.arange(N_DP, dtype=jnp.int32))
        grads = grad_acc.astype(jnp.bfloat16).reshape(3, D, GROUP, HID_DEV).transpose(0, 2, 1, 3)
        return (token_acc, score_acc), grads

    start = (jnp.zeros((TOKENS, D), jnp.float32), jnp.zeros((copies,), jnp.float32))
    (token_acc, score_acc), stacked = lax.scan(expert_step, start, jnp.arange(EXPERTS, dtype=jnp.int32))
    grad_tokens = token_acc.astype(jnp.bfloat16)
    grad_probs = score_acc.reshape(TOKENS, TOP)
    grad_gate = stacked[:, 0].reshape(SLICES, D, HID_DEV)
    grad_up = stacked[:, 1].reshape(SLICES, D, HID_DEV)
    grad_down = stacked[:, 2].reshape(SLICES, D, HID_DEV)
    return (grad_tokens, grad_probs, grad_gate, grad_up, grad_down)
```

```python
import jax
import jax.numpy as jnp
from jax import lax
from jax.sharding import Mesh, PartitionSpec as P

GROUP = 8
CAP = 8
HID = 128
PAD = 128
F32 = jnp.float32
BF16 = jnp.bfloat16
AXES = ("e", "zp", "y", "x", "c")
SWAP = [(0, 1), (1, 0)]


def dot(a, b, dims):
    return lax.dot_general(a, b, (dims, ((), ())), preferred_element_type=F32)


def split(v):
    high = lax.reduce_precision(v, 8, 7)
    return high.astype(BF16), (v - high).astype(BF16)


def columns(v):
    high, low = split(v)
    blank = jnp.zeros((v.shape[0], PAD - 2), BF16)
    return jnp.concatenate([high[:, None], low[:, None], blank], axis=1)


def joined(cols):
    return cols[:, 0].astype(F32) + cols[:, 1].astype(F32)


def swapped(x, axis):
    return lax.all_to_all(x, axis, 0, 0, tiled=True)


def shared(x, axis):
    n = lax.axis_size(axis)
    return swapped(jnp.broadcast_to(x[None], (n,) + x.shape).reshape(n * x.shape[0], -1), axis)


def per_device(tokens, grad_out, routes, route_probs, gate_weight, up_weight, down_weight):
    count, features = tokens.shape
    experts = lax.axis_size("e")
    ny = lax.axis_size("y")
    slots = experts * CAP

    own = jnp.concatenate([gate_weight[0], up_weight[0], down_weight[0]], axis=1)
    other = lax.ppermute(own, "zp", SWAP)
    block = jnp.concatenate(
        [own[:, : 2 * HID], other[:, : 2 * HID], own[:, 2 * HID :], other[:, 2 * HID :]], axis=1
    )
    weights = lax.all_gather(block, ("x", "c"), axis=0, tiled=True)
    w_gu, w_d = weights[:, : 4 * HID], weights[:, 4 * HID :]

    ids = jnp.arange(experts, dtype=jnp.int32)
    first, second = routes[:, 0:1] == ids, routes[:, 1:2] == ids
    named = (first | second).astype(BF16)
    place = jnp.arange(count)
    before = (place[:, None] > place[None, :]).astype(BF16)
    rank = dot(before, named, ((1,), (0,))).T
    taken = (named.T[:, None, :] > 0) & (rank[:, None, :] == jnp.arange(CAP, dtype=F32)[None, :, None])
    prob = jnp.where(first, route_probs[:, 0:1], 0.0) + jnp.where(second, route_probs[:, 1:2], 0.0)
    slot_prob = jnp.sum(jnp.where(taken, prob.T[:, None, :], 0.0), axis=2).reshape(slots)
    select = taken.astype(BF16).reshape(slots, count)
    send_tok = dot(select, tokens, ((1,), (0,))).astype(BF16)
    send_grd = dot(select, grad_out, ((1,), (0,))).astype(BF16)
    send_grd = jnp.concatenate([send_grd, columns(slot_prob)], axis=1)

    rows_tok = shared(swapped(send_tok, "e"), "y")
    rows_ext = shared(swapped(send_grd, "e"), "y")
    rows_grd = rows_ext[:, :features]
    rows_prob = joined(rows_ext[:, features : features + 2])[:, None]

    gu = dot(rows_tok, w_gu, ((1,), (0,)))
    gate_pre = jnp.concatenate([gu[:, :HID], gu[:, 2 * HID : 3 * HID]], axis=1)
    up_pre = jnp.concatenate([gu[:, HID : 2 * HID], gu[:, 3 * HID :]], axis=1)
    sig = jax.nn.sigmoid(gate_pre)
    act = gate_pre * sig
    hidden = (act * up_pre).astype(BF16)
    scaled = (rows_prob * rows_grd.astype(F32)).astype(BF16)
    down_grad = dot(rows_grd, w_d, ((1,), (0,)))
    scores = jnp.sum(hidden.astype(F32) * down_grad, axis=1)
    hidden_grad = rows_prob * down_grad
    gate_grad = (hidden_grad * up_pre * sig * (1.0 + gate_pre * (1.0 - sig))).astype(BF16)
    up_grad = (hidden_grad * act).astype(BF16)
    gu_grad = jnp.concatenate(
        [gate_grad[:, :HID], up_grad[:, :HID], gate_grad[:, HID:], up_grad[:, HID:]], axis=1
    )
    part = dot(gu_grad, w_gu, ((1,), (1,))).astype(BF16)
    part = jnp.concatenate([part, columns(scores)], axis=1)

    term_gu = dot(rows_tok, gu_grad, ((0,), (0,))).astype(BF16)
    term_d = dot(scaled, hidden, ((0,), (0,))).astype(BF16)
    terms = jnp.concatenate([term_gu, term_d], axis=1)
    sums = lax.psum_scatter(terms, ("x", "c"), scatter_dimension=0, tiled=True)
    keep = jnp.concatenate([sums[:, : 2 * HID], sums[:, 4 * HID : 5 * HID]], axis=1)
    give = jnp.concatenate([sums[:, 2 * HID : 4 * HID], sums[:, 5 * HID :]], axis=1)
    grads = (keep.astype(F32) + lax.ppermute(give, "zp", SWAP).astype(F32)).astype(BF16)

    back = jnp.sum(swapped(part, "y").astype(F32).reshape(ny, slots, -1), axis=0)
    back_score = columns(joined(back[:, features : features + 2]))
    back = jnp.concatenate([back[:, :features].astype(BF16), back_score], axis=1)
    back = swapped(back, "e")
    grad_tokens = dot(select, back[:, :features], ((0,), (0,))).astype(BF16)
    score = joined(back[:, features : features + 2]).reshape(experts, CAP, 1)
    score = jnp.sum(jnp.where(taken, score, 0.0), axis=1).T
    grad_probs = jnp.stack(
        [jnp.sum(jnp.where(first, score, 0.0), axis=1), jnp.sum(jnp.where(second, score, 0.0), axis=1)], axis=1
    )
    return (
        grad_tokens,
        grad_probs,
        grads[None, :, :HID],
        grads[None, :, HID : 2 * HID],
        grads[None, :, 2 * HID :],
    )


def solution(mesh):
    fine = Mesh(mesh.devices.reshape(mesh.shape["ep"] // GROUP, 2, GROUP // 2, -1, 2), AXES)
    rows, stored = P(AXES, None), P(AXES[:3], AXES[3:], None)
    return jax.shard_map(
        per_device,
        mesh=fine,
        in_specs=(rows, rows, rows, rows, stored, stored, stored),
        out_specs=(rows, rows, stored, stored, stored),
        check_vma=False,
    )
```

```python
import functools

import jax
import jax.numpy as jnp
from jax import lax
from jax.experimental import pallas as pl
from jax.experimental.pallas import tpu as pltpu
from jax.sharding import Mesh, PartitionSpec as P


GROUP = 8
CAP = 8
HID = 128
PAD = 128
F32 = jnp.float32
BF16 = jnp.bfloat16
AXES = ("e", "zp", "y", "x", "c")
HOLD = ("zp", "x", "c")
KINDS = 3


def dot(a, b, dims):
    return lax.dot_general(a, b, (dims, ((), ())), preferred_element_type=F32)


def split(v):
    high = lax.reduce_precision(v, 8, 7)
    return high.astype(BF16), (v - high).astype(BF16)


def columns(v):
    high, low = split(v)
    blank = jnp.zeros((v.shape[0], PAD - 2), BF16)
    return jnp.concatenate([high[:, None], low[:, None], blank], axis=1)


def joined(cols):
    return cols[:, 0].astype(F32) + cols[:, 1].astype(F32)


def swapped(x, axis):
    return lax.all_to_all(x, axis, 0, 0, tiled=True)


def shared(x, axis):
    n = lax.axis_size(axis)
    return swapped(jnp.broadcast_to(x[None], (n,) + x.shape).reshape(n * x.shape[0], -1), axis)


def expert_kernel(nz, nx, tok_hbm, ext_hbm, w_hbm, terms_hbm, part_hbm,
                  tok, ext, w, terms, part, gu_acc, d_acc, row_sem, w_sem, terms_sem, part_sem):
    features = tok.shape[1]
    chunk = features // nx
    piece = chunk // 2

    def pieces(x):
        for z in range(nz):
            for c in range(2):
                for m in range(KINDS):
                    yield ((z * nx + x) * 2 + c) * KINDS + m, x * chunk + c * piece, (m * nz + z) * HID

    load_tok = pltpu.make_async_copy(tok_hbm, tok, row_sem.at[0])
    load_ext = pltpu.make_async_copy(ext_hbm, ext, row_sem.at[1])
    load_tok.start()
    loads = []
    for x in range(nx):
        if x == 1:
            load_ext.start()
        loads.append([])
        for i, row, col in pieces(x):
            copy = pltpu.make_async_copy(
                w_hbm.at[pl.ds(i * piece, piece), :],
                w.at[pl.ds(row, piece), pl.ds(col, HID)],
                w_sem.at[i],
            )
            copy.start()
            loads[-1].append(copy)
    wide = nz * HID
    load_tok.wait()
    for x in range(nx):
        for copy in loads[x]:
            copy.wait()
        if x == 0:
            load_ext.wait()
        span = slice(x * chunk, (x + 1) * chunk)
        gu = dot(tok[:, span], w[span, : 2 * wide], ((1,), (0,)))
        dg = dot(ext[:, span], w[span, 2 * wide :], ((1,), (0,)))
        if x == 0:
            gu_acc[...] = gu
            d_acc[...] = dg
        else:
            gu_acc[...] += gu
            d_acc[...] += dg
    extra = ext[:, features:].astype(F32)
    prob = extra[:, 0:1] + extra[:, 1:2]
    gate_pre, up_pre = gu_acc[:, :wide], gu_acc[:, wide:]
    down_grad = d_acc[...]
    sig = jax.nn.sigmoid(gate_pre)
    act = gate_pre * sig
    hidden = (act * up_pre).astype(BF16)
    scores = jnp.sum(hidden.astype(F32) * down_grad, axis=1, keepdims=True)
    hidden_grad = prob * down_grad
    gate_grad = (hidden_grad * up_pre * sig * (1.0 + gate_pre * (1.0 - sig))).astype(BF16)
    up_grad = (hidden_grad * act).astype(BF16)
    gu_grad = jnp.concatenate([gate_grad, up_grad], axis=1)
    stores = []
    for x in range(nx):
        span = slice(x * chunk, (x + 1) * chunk)
        terms[span, : 2 * wide] = dot(tok[:, span], gu_grad, ((0,), (0,))).astype(BF16)
        scaled = (prob * ext[:, span].astype(F32)).astype(BF16)
        terms[span, 2 * wide :] = dot(scaled, hidden, ((0,), (0,))).astype(BF16)
        for i, row, col in pieces(x):
            copy = pltpu.make_async_copy(
                terms.at[pl.ds(row, piece), pl.ds(col, HID)],
                terms_hbm.at[pl.ds(i * piece, piece), :],
                terms_sem.at[i],
            )
            copy.start()
            stores.append(copy)
    lane = lax.broadcasted_iota(jnp.int32, (scores.shape[0], PAD), 1)
    high = scores.astype(BF16).astype(F32)
    low = scores - high
    part[:, features:] = jnp.where(lane == 0, high, jnp.where(lane == 1, low, 0.0)).astype(BF16)
    for x in range(nx):
        span = slice(x * chunk, (x + 1) * chunk)
        part[:, span] = dot(gu_grad, w[span, : 2 * wide], ((1,), (1,))).astype(BF16)
        if x == nx - 1:
            span = slice(x * chunk, features + PAD)
        copy = pltpu.make_async_copy(part.at[:, span], part_hbm.at[:, span], part_sem.at[x])
        copy.start()
        stores.append(copy)
    for copy in stores:
        copy.wait()


def expert_math(tok, ext, w, nz, nx):
    rows, features = tok.shape
    held = w.shape[0]
    wide = nz * HID
    spec = pl.BlockSpec(memory_space=pl.ANY)
    count = nz * nx * 2 * KINDS
    return pl.pallas_call(
        functools.partial(expert_kernel, nz, nx),
        name="expert_math",
        out_shape=(
            jax.ShapeDtypeStruct((held, HID), BF16),
            jax.ShapeDtypeStruct((rows, features + PAD), BF16),
        ),
        in_specs=[spec] * 3,
        out_specs=(spec, spec),
        scratch_shapes=[
            pltpu.VMEM((rows, features), BF16),
            pltpu.VMEM((rows, features + PAD), BF16),
            pltpu.VMEM((features, KINDS * wide), BF16),
            pltpu.VMEM((features, KINDS * wide), BF16),
            pltpu.VMEM((rows, features + PAD), BF16),
            pltpu.VMEM((rows, 2 * wide), F32),
            pltpu.VMEM((rows, wide), F32),
            pltpu.SemaphoreType.DMA((2,)),
            pltpu.SemaphoreType.DMA((count,)),
            pltpu.SemaphoreType.DMA((count,)),
            pltpu.SemaphoreType.DMA((nx,)),
        ],
        cost_estimate=pl.CostEstimate(
            flops=16 * rows * features * wide,
            transcendentals=rows * wide,
            bytes_accessed=2 * (2 * held * HID + 3 * rows * features),
        ),
    )(tok, ext, w)


def layer(tokens, grad_out, routes, route_probs, gate_weight, up_weight, down_weight):
    count, features = tokens.shape
    experts, ny = lax.axis_size("e"), lax.axis_size("y")
    nz, nx = lax.axis_size("zp"), lax.axis_size("x")
    slots = experts * CAP

    stored = jnp.concatenate([gate_weight[0], up_weight[0], down_weight[0]], axis=0)
    weights = lax.all_gather(stored, HOLD, axis=0, tiled=True)

    ids = jnp.arange(experts, dtype=jnp.int32)
    first, second = routes[:, 0:1] == ids, routes[:, 1:2] == ids
    named = (first | second).astype(BF16)
    place = jnp.arange(count)
    before = (place[:, None] > place[None, :]).astype(BF16)
    rank = dot(before, named, ((1,), (0,))).T
    taken = (named.T[:, None, :] > 0) & (rank[:, None, :] == jnp.arange(CAP, dtype=F32)[None, :, None])
    prob = jnp.where(first, route_probs[:, 0:1], 0.0) + jnp.where(second, route_probs[:, 1:2], 0.0)
    slot_prob = jnp.sum(jnp.where(taken, prob.T[:, None, :], 0.0), axis=2).reshape(slots)
    select = taken.astype(BF16).reshape(slots, count)
    send_tok = dot(select, tokens, ((1,), (0,))).astype(BF16)
    send_grd = dot(select, grad_out, ((1,), (0,))).astype(BF16)
    send_grd = jnp.concatenate([send_grd, columns(slot_prob)], axis=1)

    came_tok = swapped(send_tok, "e")
    came_tok, send_grd = lax.optimization_barrier((came_tok, send_grd))
    rows_tok = lax.all_gather(came_tok, "y", axis=0, tiled=True)
    rows_ext = shared(swapped(send_grd, "e"), "y")

    terms, part = expert_math(rows_tok, rows_ext, weights, nz, nx)
    sums = lax.psum_scatter(terms, HOLD, scatter_dimension=0, tiled=True)
    grads = sums.reshape(KINDS, 1, -1, HID)

    back = jnp.sum(swapped(part, "y").astype(F32).reshape(ny, slots, -1), axis=0)
    back_score = columns(joined(back[:, features : features + 2]))
    back = jnp.concatenate([back[:, :features].astype(BF16), back_score], axis=1)
    back = swapped(back, "e")
    grad_tokens = dot(select, back[:, :features], ((0,), (0,))).astype(BF16)
    score = joined(back[:, features : features + 2]).reshape(experts, CAP, 1)
    score = jnp.sum(jnp.where(taken, score, 0.0), axis=1).T
    grad_probs = jnp.stack(
        [jnp.sum(jnp.where(first, score, 0.0), axis=1), jnp.sum(jnp.where(second, score, 0.0), axis=1)], axis=1
    )
    return (grad_tokens, grad_probs, grads[0], grads[1], grads[2])


def solution(mesh):
    fine = Mesh(mesh.devices.reshape(mesh.shape["ep"] // GROUP, 2, GROUP // 2, -1, 2), AXES)
    rows, stored = P(AXES, None), P(AXES[:3], AXES[3:], None)
    return jax.shard_map(
        layer,
        mesh=fine,
        in_specs=(rows, rows, rows, rows, stored, stored, stored),
        out_specs=(rows, rows, stored, stored, stored),
        check_vma=False,
    )
```

```python
import functools

import jax
import jax.numpy as jnp
from jax import lax
from jax.experimental import pallas as pl
from jax.experimental.pallas import tpu as pltpu
from jax.sharding import Mesh, PartitionSpec as P


GROUP = 8
CAP = 8
HID = 128
PAD = 128
F32 = jnp.float32
BF16 = jnp.bfloat16
AXES = ("e", "zp", "y", "x", "c")
HOLD = ("x", "c")
SWAP = [(0, 1), (1, 0)]
KINDS = 3


def dot(a, b, dims):
    return lax.dot_general(a, b, (dims, ((), ())), preferred_element_type=F32)


def split(v):
    high = lax.reduce_precision(v, 8, 7)
    return high.astype(BF16), (v - high).astype(BF16)


def columns(v):
    high, low = split(v)
    blank = jnp.zeros((v.shape[0], PAD - 2), BF16)
    return jnp.concatenate([high[:, None], low[:, None], blank], axis=1)


def joined(cols):
    return cols[:, 0].astype(F32) + cols[:, 1].astype(F32)


def swapped(x, axis):
    return lax.all_to_all(x, axis, 0, 0, tiled=True)


def shared(x, axis):
    n = lax.axis_size(axis)
    return swapped(jnp.broadcast_to(x[None], (n,) + x.shape).reshape(n * x.shape[0], -1), axis)


def expert_kernel(nz, nx, ny, y_ref, own_hbm, left_hbm, right_hbm, fara_hbm, farb_hbm, ext_hbm, w_hbm, terms_hbm, part_hbm,
                  tok, ext, w, terms, part, gu_acc, d_acc, row_sem, w_sem, terms_sem, part_sem):
    features = tok.shape[1]
    chunk = features // nx
    piece = chunk // 2

    def pieces(x):
        for z in range(nz):
            for c in range(2):
                for m in range(KINDS):
                    yield ((x * 2 + c) * nz + z) * KINDS + m, x * chunk + c * piece, (m * nz + z) * HID

    block = own_hbm.shape[0]
    half = fara_hbm.shape[0]
    load_tok = []
    for n, (source, ahead, skip) in enumerate(
        ((own_hbm, 0, 0), (left_hbm, ny - 1, 0), (right_hbm, 1, 0), (fara_hbm, 2, 0), (farb_hbm, 2, half))
    ):
        at = pl.multiple_of(lax.rem(y_ref[0] + ahead, ny) * block + skip, half)
        load_tok.append(pltpu.make_async_copy(source, tok.at[pl.ds(at, source.shape[0]), :], row_sem.at[n]))
        load_tok[-1].start()
    load_ext = pltpu.make_async_copy(ext_hbm, ext, row_sem.at[5])
    loads = []
    for x in range(nx):
        if x == 1:
            load_ext.start()
        loads.append([])
        for i, row, col in pieces(x):
            copy = pltpu.make_async_copy(
                w_hbm.at[pl.ds(i * piece, piece), :],
                w.at[pl.ds(row, piece), pl.ds(col, HID)],
                w_sem.at[i],
            )
            copy.start()
            loads[-1].append(copy)
    wide = nz * HID
    for copy in load_tok:
        copy.wait()
    for x in range(nx):
        for copy in loads[x]:
            copy.wait()
        if x == 0:
            load_ext.wait()
        span = slice(x * chunk, (x + 1) * chunk)
        gu = dot(tok[:, span], w[span, : 2 * wide], ((1,), (0,)))
        dg = dot(ext[:, span], w[span, 2 * wide :], ((1,), (0,)))
        if x == 0:
            gu_acc[...] = gu
            d_acc[...] = dg
        else:
            gu_acc[...] += gu
            d_acc[...] += dg
    extra = ext[:, features:].astype(F32)
    prob = extra[:, 0:1] + extra[:, 1:2]
    gate_pre, up_pre = gu_acc[:, :wide], gu_acc[:, wide:]
    down_grad = d_acc[...]
    sig = jax.nn.sigmoid(gate_pre)
    act = gate_pre * sig
    hidden = (act * up_pre).astype(BF16)
    scores = jnp.sum(hidden.astype(F32) * down_grad, axis=1, keepdims=True)
    hidden_grad = prob * down_grad
    gate_grad = (hidden_grad * up_pre * sig * (1.0 + gate_pre * (1.0 - sig))).astype(BF16)
    up_grad = (hidden_grad * act).astype(BF16)
    gu_grad = jnp.concatenate([gate_grad, up_grad], axis=1)
    stores = []
    for x in range(nx):
        span = slice(x * chunk, (x + 1) * chunk)
        terms[span, : 2 * wide] = dot(tok[:, span], gu_grad, ((0,), (0,))).astype(BF16)
        scaled = (prob * ext[:, span].astype(F32)).astype(BF16)
        terms[span, 2 * wide :] = dot(scaled, hidden, ((0,), (0,))).astype(BF16)
        for i, row, col in pieces(x):
            copy = pltpu.make_async_copy(
                terms.at[pl.ds(row, piece), pl.ds(col, HID)],
                terms_hbm.at[pl.ds(i * piece, piece), :],
                terms_sem.at[i],
            )
            copy.start()
            stores.append(copy)
    lane = lax.broadcasted_iota(jnp.int32, (scores.shape[0], PAD), 1)
    high = scores.astype(BF16).astype(F32)
    low = scores - high
    part[:, features:] = jnp.where(lane == 0, high, jnp.where(lane == 1, low, 0.0)).astype(BF16)
    for x in range(nx):
        span = slice(x * chunk, (x + 1) * chunk)
        part[:, span] = dot(gu_grad, w[span, : 2 * wide], ((1,), (1,))).astype(BF16)
        if x == nx - 1:
            span = slice(x * chunk, features + PAD)
        copy = pltpu.make_async_copy(part.at[:, span], part_hbm.at[:, span], part_sem.at[x])
        copy.start()
        stores.append(copy)
    for copy in stores:
        copy.wait()


def expert_math(y, tok, ext, w, nz, nx):
    rows, features = ext.shape[0], ext.shape[1] - PAD
    ny = rows // tok[0].shape[0]
    held = w.shape[0]
    wide = nz * HID
    spec = pl.BlockSpec(memory_space=pl.ANY)
    count = nz * nx * 2 * KINDS
    return pl.pallas_call(
        functools.partial(expert_kernel, nz, nx, ny),
        name="expert_math",
        out_shape=(
            jax.ShapeDtypeStruct((held, HID), BF16),
            jax.ShapeDtypeStruct((rows, features + PAD), BF16),
        ),
        in_specs=[pl.BlockSpec(memory_space=pltpu.SMEM)] + [spec] * (len(tok) + 2),
        out_specs=(spec, spec),
        scratch_shapes=[
            pltpu.VMEM((rows, features), BF16),
            pltpu.VMEM((rows, features + PAD), BF16),
            pltpu.VMEM((features, KINDS * wide), BF16),
            pltpu.VMEM((features, KINDS * wide), BF16),
            pltpu.VMEM((rows, features + PAD), BF16),
            pltpu.VMEM((rows, 2 * wide), F32),
            pltpu.VMEM((rows, wide), F32),
            pltpu.SemaphoreType.DMA((6,)),
            pltpu.SemaphoreType.DMA((count,)),
            pltpu.SemaphoreType.DMA((count,)),
            pltpu.SemaphoreType.DMA((nx,)),
        ],
        cost_estimate=pl.CostEstimate(
            flops=16 * rows * features * wide,
            transcendentals=rows * wide,
            bytes_accessed=2 * (2 * held * HID + 3 * rows * features),
        ),
    )(y, *tok, ext, w)


def layer(tokens, grad_out, routes, route_probs, gate_weight, up_weight, down_weight):
    count, features = tokens.shape
    experts, ny = lax.axis_size("e"), lax.axis_size("y")
    nz, nx = lax.axis_size("zp"), lax.axis_size("x")
    slots = experts * CAP

    stored = jnp.concatenate([gate_weight[0], up_weight[0], down_weight[0]], axis=0)
    paired = lax.ppermute(stored, "zp", SWAP)
    weights = lax.all_gather(jnp.concatenate([stored, paired], axis=0), HOLD, axis=0, tiled=True)

    ids = jnp.arange(experts, dtype=jnp.int32)
    first, second = routes[:, 0:1] == ids, routes[:, 1:2] == ids
    named = (first | second).astype(BF16)
    place = jnp.arange(count)
    before = (place[:, None] > place[None, :]).astype(BF16)
    rank = dot(before, named, ((1,), (0,))).T
    taken = (named.T[:, None, :] > 0) & (rank[:, None, :] == jnp.arange(CAP, dtype=F32)[None, :, None])
    prob = jnp.where(first, route_probs[:, 0:1], 0.0) + jnp.where(second, route_probs[:, 1:2], 0.0)
    slot_prob = jnp.sum(jnp.where(taken, prob.T[:, None, :], 0.0), axis=2).reshape(slots)
    select = taken.astype(BF16).reshape(slots, count)
    send_tok = dot(select, tokens, ((1,), (0,))).astype(BF16)
    send_grd = dot(select, grad_out, ((1,), (0,))).astype(BF16)
    send_grd = jnp.concatenate([send_grd, columns(slot_prob)], axis=1)

    own = swapped(send_tok, "e")
    own, send_grd = lax.optimization_barrier((own, send_grd))
    up, down = [(i, (i + 1) % ny) for i in range(ny)], [(i, (i - 1) % ny) for i in range(ny)]
    half = slots // 2
    left, right = lax.ppermute(own, "y", up), lax.ppermute(own, "y", down)
    far = lax.ppermute(left[:half], "y", up), lax.ppermute(right[half:], "y", down)
    came_grd = swapped(send_grd, "e")
    rows_ext = shared(came_grd, "y")

    y = lax.axis_index("y").astype(jnp.int32).reshape(1)
    terms, part = expert_math(y, (own, left, right) + far, rows_ext, weights, nz, nx)
    sums = lax.psum_scatter(terms, HOLD, scatter_dimension=0, tiled=True)
    kept, given = jnp.split(sums, 2, axis=0)
    given = lax.ppermute(given, "zp", SWAP)
    grads = (kept.astype(F32) + given.astype(F32)).astype(BF16).reshape(KINDS, 1, -1, HID)

    back = jnp.sum(swapped(part, "y").astype(F32).reshape(ny, slots, -1), axis=0)
    back_score = columns(joined(back[:, features : features + 2]))
    back = jnp.concatenate([back[:, :features].astype(BF16), back_score], axis=1)
    back = swapped(back, "e")
    grad_tokens = dot(select, back[:, :features], ((0,), (0,))).astype(BF16)
    score = joined(back[:, features : features + 2]).reshape(experts, CAP, 1)
    score = jnp.sum(jnp.where(taken, score, 0.0), axis=1).T
    grad_probs = jnp.stack(
        [jnp.sum(jnp.where(first, score, 0.0), axis=1), jnp.sum(jnp.where(second, score, 0.0), axis=1)], axis=1
    )
    return (grad_tokens, grad_probs, grads[0], grads[1], grads[2])


def solution(mesh):
    fine = Mesh(mesh.devices.reshape(mesh.shape["ep"] // GROUP, 2, GROUP // 2, -1, 2), AXES)
    rows, stored = P(AXES, None), P(AXES[:3], AXES[3:], None)
    return jax.shard_map(
        layer,
        mesh=fine,
        in_specs=(rows, rows, rows, rows, stored, stored, stored),
        out_specs=(rows, rows, stored, stored, stored),
        check_vma=False,
    )
```

```python
import functools

import jax
import jax.numpy as jnp
from jax import lax
from jax.experimental import pallas as pl
from jax.experimental.pallas import tpu as pltpu
from jax.sharding import Mesh, PartitionSpec as P


GROUP = 8
CAP = 8
HID = 128
PAD = 128
F32 = jnp.float32
BF16 = jnp.bfloat16
AXES = ("e", "zp", "y", "x", "c")
HOLD = ("x", "c")
SWAP = [(0, 1), (1, 0)]
KINDS = 3


def dot(a, b, dims):
    return lax.dot_general(a, b, (dims, ((), ())), preferred_element_type=F32)


def split(v):
    high = lax.reduce_precision(v, 8, 7)
    return high.astype(BF16), (v - high).astype(BF16)


def columns(v):
    high, low = split(v)
    blank = jnp.zeros((v.shape[0], PAD - 2), BF16)
    return jnp.concatenate([high[:, None], low[:, None], blank], axis=1)


def joined(cols):
    return cols[:, 0].astype(F32) + cols[:, 1].astype(F32)


def swapped(x, axis):
    return lax.all_to_all(x, axis, 0, 0, tiled=True)


def shared(x, axis):
    n = lax.axis_size(axis)
    return swapped(jnp.broadcast_to(x[None], (n,) + x.shape).reshape(n * x.shape[0], -1), axis)


def pieces(nz, nx, x, features):
    chunk = features // nx
    piece = chunk // 2
    for c in range(2):
        for z in range(nz):
            for m in range(KINDS):
                yield m, ((x * 2 + c) * nz + z) * KINDS + m, x * chunk + c * piece, (m * nz + z) * HID


def load_weights(nz, nx, features, w_hbm, w, sem, kinds):
    piece = features // nx // 2
    loads = []
    for x in range(nx):
        loads.append([])
        for m, i, row, col in pieces(nz, nx, x, features):
            if m in kinds:
                copy = pltpu.make_async_copy(
                    w_hbm.at[pl.ds(i * piece, piece), :],
                    w.at[pl.ds(row, piece), pl.ds(col, HID)],
                    sem.at[i],
                )
                copy.start()
                loads[-1].append(copy)
    return loads


def load_rows(ny, y_ref, sources, rows, sem):
    own = sources[0]
    block, half = own.shape[0], sources[3].shape[0]
    loads = []
    for n, (ahead, skip) in enumerate(((0, 0), (ny - 1, 0), (1, 0), (2, 0), (2, half))):
        at = pl.multiple_of(lax.rem(y_ref[0] + ahead, ny) * block + skip, half)
        source = sources[n]
        loads.append(pltpu.make_async_copy(source, rows.at[pl.ds(at, source.shape[0]), :], sem.at[n]))
        loads[-1].start()
    return loads


def pre_kernel(nz, nx, ny, y_ref, s0, s1, s2, s3, s4, w_hbm, gu_ref, tok, w, row_sem, w_sem):
    features = tok.shape[1]
    chunk = features // nx
    rows = load_rows(ny, y_ref, (s0, s1, s2, s3, s4), tok, row_sem)
    loads = load_weights(nz, nx, features, w_hbm, w, w_sem, (0, 1))
    for copy in rows:
        copy.wait()
    for x in range(nx):
        for copy in loads[x]:
            copy.wait()
        span = slice(x * chunk, (x + 1) * chunk)
        gu = dot(tok[:, span], w[span, :], ((1,), (0,)))
        if x == 0:
            gu_ref[...] = gu
        else:
            gu_ref[...] += gu


def expert_kernel(nz, nx, ny, y_ref, s0, s1, s2, s3, s4, low_hbm, high_hbm, w_hbm, gu_ref, terms_hbm, part_hbm,
                  tok, ext, w, terms, part, d_acc, row_sem, w_sem, terms_sem, part_sem):
    features = tok.shape[1]
    chunk = features // nx
    piece = chunk // 2
    cut = low_hbm.shape[1]
    wide = nz * HID
    load_low = pltpu.make_async_copy(low_hbm, ext.at[:, pl.ds(0, cut)], row_sem.at[5])
    load_high = pltpu.make_async_copy(high_hbm, ext.at[:, pl.ds(cut, high_hbm.shape[1])], row_sem.at[6])
    load_low.start()
    loads_d = load_weights(nz, nx, features, w_hbm, w, w_sem, (2,))
    load_high.start()
    rows = load_rows(ny, y_ref, (s0, s1, s2, s3, s4), tok, row_sem)
    loads = load_weights(nz, nx, features, w_hbm, w, w_sem, (0, 1))
    load_low.wait()
    for x in range(nx):
        if x * 2 == nx:
            load_high.wait()
        for copy in loads_d[x]:
            copy.wait()
        span = slice(x * chunk, (x + 1) * chunk)
        dg = dot(ext[:, span], w[span, 2 * wide :], ((1,), (0,)))
        if x == 0:
            d_acc[...] = dg
        else:
            d_acc[...] += dg
    extra = ext[:, features:].astype(F32)
    prob = extra[:, 0:1] + extra[:, 1:2]
    gate_pre, up_pre = gu_ref[:, :wide], gu_ref[:, wide:]
    down_grad = d_acc[...]
    sig = jax.nn.sigmoid(gate_pre)
    act = gate_pre * sig
    hidden = (act * up_pre).astype(BF16)
    scores = jnp.sum(hidden.astype(F32) * down_grad, axis=1, keepdims=True)
    hidden_grad = prob * down_grad
    gate_grad = (hidden_grad * up_pre * sig * (1.0 + gate_pre * (1.0 - sig))).astype(BF16)
    up_grad = (hidden_grad * act).astype(BF16)
    gu_grad = jnp.concatenate([gate_grad, up_grad], axis=1)
    for copy in rows:
        copy.wait()
    stores = []
    for x in range(nx):
        span = slice(x * chunk, (x + 1) * chunk)
        terms[span, : 2 * wide] = dot(tok[:, span], gu_grad, ((0,), (0,))).astype(BF16)
        scaled = (prob * ext[:, span].astype(F32)).astype(BF16)
        terms[span, 2 * wide :] = dot(scaled, hidden, ((0,), (0,))).astype(BF16)
        for m, i, row, col in pieces(nz, nx, x, features):
            copy = pltpu.make_async_copy(
                terms.at[pl.ds(row, piece), pl.ds(col, HID)],
                terms_hbm.at[pl.ds(i * piece, piece), :],
                terms_sem.at[i],
            )
            copy.start()
            stores.append(copy)
    lane = lax.broadcasted_iota(jnp.int32, (scores.shape[0], PAD), 1)
    high = scores.astype(BF16).astype(F32)
    low = scores - high
    part[:, features:] = jnp.where(lane == 0, high, jnp.where(lane == 1, low, 0.0)).astype(BF16)
    for x in range(nx):
        for copy in loads[x]:
            copy.wait()
        span = slice(x * chunk, (x + 1) * chunk)
        part[:, span] = dot(gu_grad, w[span, : 2 * wide], ((1,), (1,))).astype(BF16)
        if x == nx - 1:
            span = slice(x * chunk, features + PAD)
        copy = pltpu.make_async_copy(part.at[:, span], part_hbm.at[:, span], part_sem.at[x])
        copy.start()
        stores.append(copy)
    for copy in stores:
        copy.wait()


ANYWHERE = pl.BlockSpec(memory_space=pl.ANY)
SCALAR = pl.BlockSpec(memory_space=pltpu.SMEM)
INSIDE = pl.BlockSpec(memory_space=pltpu.VMEM)


def pre_math(y, tok, w, rows, nz, nx):
    features = tok[0].shape[1]
    wide = nz * HID
    count = nz * nx * 2 * KINDS
    return pl.pallas_call(
        functools.partial(pre_kernel, nz, nx, rows // tok[0].shape[0]),
        name="pre_math",
        out_shape=jax.ShapeDtypeStruct((rows, 2 * wide), F32),
        in_specs=[SCALAR] + [ANYWHERE] * (len(tok) + 1),
        out_specs=INSIDE,
        scratch_shapes=[
            pltpu.VMEM((rows, features), BF16),
            pltpu.VMEM((features, 2 * wide), BF16),
            pltpu.SemaphoreType.DMA((5,)),
            pltpu.SemaphoreType.DMA((count,)),
        ],
        cost_estimate=pl.CostEstimate(
            flops=4 * rows * features * wide,
            transcendentals=0,
            bytes_accessed=2 * features * (2 * wide + rows),
        ),
    )(y, *tok, w)


def expert_math(y, tok, low, high, w, gu, nz, nx):
    rows, features = low.shape[0], tok[0].shape[1]
    held = w.shape[0]
    wide = nz * HID
    count = nz * nx * 2 * KINDS
    return pl.pallas_call(
        functools.partial(expert_kernel, nz, nx, rows // tok[0].shape[0]),
        name="expert_math",
        out_shape=(
            jax.ShapeDtypeStruct((held, HID), BF16),
            jax.ShapeDtypeStruct((rows, features + PAD), BF16),
        ),
        in_specs=[SCALAR] + [ANYWHERE] * (len(tok) + 3) + [INSIDE],
        out_specs=(ANYWHERE, ANYWHERE),
        scratch_shapes=[
            pltpu.VMEM((rows, features), BF16),
            pltpu.VMEM((rows, features + PAD), BF16),
            pltpu.VMEM((features, KINDS * wide), BF16),
            pltpu.VMEM((features, KINDS * wide), BF16),
            pltpu.VMEM((rows, features + PAD), BF16),
            pltpu.VMEM((rows, wide), F32),
            pltpu.SemaphoreType.DMA((7,)),
            pltpu.SemaphoreType.DMA((count,)),
            pltpu.SemaphoreType.DMA((count,)),
            pltpu.SemaphoreType.DMA((nx,)),
        ],
        cost_estimate=pl.CostEstimate(
            flops=12 * rows * features * wide,
            transcendentals=rows * wide,
            bytes_accessed=2 * (2 * held * HID + 3 * rows * features),
        ),
    )(y, *tok, low, high, w, gu)


def layer(tokens, grad_out, routes, route_probs, gate_weight, up_weight, down_weight):
    count, features = tokens.shape
    experts, ny = lax.axis_size("e"), lax.axis_size("y")
    nz, nx = lax.axis_size("zp"), lax.axis_size("x")
    slots = experts * CAP

    stored = jnp.concatenate([gate_weight[0], up_weight[0], down_weight[0]], axis=0)
    paired = lax.ppermute(stored, "zp", SWAP)
    weights = lax.all_gather(jnp.concatenate([stored, paired], axis=0), HOLD, axis=0, tiled=True)

    ids = jnp.arange(experts, dtype=jnp.int32)
    first, second = routes[:, 0:1] == ids, routes[:, 1:2] == ids
    named = (first | second).astype(BF16)
    place = jnp.arange(count)
    before = (place[:, None] > place[None, :]).astype(BF16)
    rank = dot(before, named, ((1,), (0,))).T
    taken = (named.T[:, None, :] > 0) & (rank[:, None, :] == jnp.arange(CAP, dtype=F32)[None, :, None])
    prob = jnp.where(first, route_probs[:, 0:1], 0.0) + jnp.where(second, route_probs[:, 1:2], 0.0)
    slot_prob = jnp.sum(jnp.where(taken, prob.T[:, None, :], 0.0), axis=2).reshape(slots)
    select = taken.astype(BF16).reshape(slots, count)
    send_tok = dot(select, tokens, ((1,), (0,))).astype(BF16)
    send_grd = dot(select, grad_out, ((1,), (0,))).astype(BF16)
    send_grd = jnp.concatenate([send_grd, columns(slot_prob)], axis=1)

    own = swapped(send_tok, "e")
    own, send_grd = lax.optimization_barrier((own, send_grd))
    up, down = [(i, (i + 1) % ny) for i in range(ny)], [(i, (i - 1) % ny) for i in range(ny)]
    half = slots // 2
    left, right = lax.ppermute(own, "y", up), lax.ppermute(own, "y", down)
    halves = left[:half], right[half:]
    far = lax.ppermute(halves[0], "y", up), lax.ppermute(halves[1], "y", down)
    came_grd = swapped(send_grd, "e")
    cut = features * 3 // 7
    rows_high = lax.all_gather(came_grd[:, cut:], "y", axis=0, tiled=True)
    rows_low = shared(came_grd[:, :cut], "y")

    y = lax.axis_index("y").astype(jnp.int32).reshape(1)
    tok = (own, left, right) + far
    gate_up = pre_math(y, tok, weights, ny * slots, nz, nx)
    terms, part = expert_math(y, tok, rows_low, rows_high, weights, gate_up, nz, nx)
    sums = lax.psum_scatter(terms, HOLD, scatter_dimension=0, tiled=True)
    kept, given = jnp.split(sums, 2, axis=0)
    given = lax.ppermute(given, "zp", SWAP)
    grads = (kept.astype(F32) + given.astype(F32)).astype(BF16).reshape(KINDS, 1, -1, HID)

    back = jnp.sum(swapped(part, "y").astype(F32).reshape(ny, slots, -1), axis=0)
    back_score = columns(joined(back[:, features : features + 2]))
    back = jnp.concatenate([back[:, :features].astype(BF16), back_score], axis=1)
    back = swapped(back, "e")
    grad_tokens = dot(select, back[:, :features], ((0,), (0,))).astype(BF16)
    score = joined(back[:, features : features + 2]).reshape(experts, CAP, 1)
    score = jnp.sum(jnp.where(taken, score, 0.0), axis=1).T
    grad_probs = jnp.stack(
        [jnp.sum(jnp.where(first, score, 0.0), axis=1), jnp.sum(jnp.where(second, score, 0.0), axis=1)], axis=1
    )
    return (grad_tokens, grad_probs, grads[0], grads[1], grads[2])


def solution(mesh):
    fine = Mesh(mesh.devices.reshape(mesh.shape["ep"] // GROUP, 2, GROUP // 2, -1, 2), AXES)
    rows, stored = P(AXES, None), P(AXES[:3], AXES[3:], None)
    return jax.shard_map(
        layer,
        mesh=fine,
        in_specs=(rows, rows, rows, rows, stored, stored, stored),
        out_specs=(rows, rows, stored, stored, stored),
        check_vma=False,
    )
```

```python
import functools

import jax
import jax.numpy as jnp
from jax import lax
from jax.experimental import pallas as pl
from jax.experimental.pallas import tpu as pltpu
from jax.sharding import Mesh, PartitionSpec as P


GROUP = 8
CAP = 8
HID = 128
PAD = 128
F32 = jnp.float32
BF16 = jnp.bfloat16
AXES = ("e", "zp", "y", "x", "c")
HOLD = ("x", "c")
SWAP = [(0, 1), (1, 0)]
KINDS = 3


def dot(a, b, dims):
    return lax.dot_general(a, b, (dims, ((), ())), preferred_element_type=F32)


def split(v):
    high = lax.reduce_precision(v, 8, 7)
    return high.astype(BF16), (v - high).astype(BF16)


def columns(v):
    high, low = split(v)
    blank = jnp.zeros((v.shape[0], PAD - 2), BF16)
    return jnp.concatenate([high[:, None], low[:, None], blank], axis=1)


def joined(cols):
    return cols[:, 0].astype(F32) + cols[:, 1].astype(F32)


def swapped(x, axis):
    return lax.all_to_all(x, axis, 0, 0, tiled=True)


def shared(x, axis):
    n = lax.axis_size(axis)
    return swapped(jnp.broadcast_to(x[None], (n,) + x.shape).reshape(n * x.shape[0], -1), axis)


def pieces(nz, nx, x, features):
    chunk = features // nx
    piece = chunk // 2
    for c in range(2):
        for z in range(nz):
            for m in range(KINDS):
                yield m, ((x * 2 + c) * nz + z) * KINDS + m, x * chunk + c * piece, (m * nz + z) * HID


def load_weights(nz, nx, features, w_hbm, w, sem, kinds):
    piece = features // nx // 2
    loads = []
    for x in range(nx):
        loads.append([])
        for m, i, row, col in pieces(nz, nx, x, features):
            if m in kinds:
                copy = pltpu.make_async_copy(
                    w_hbm.at[pl.ds(i * piece, piece), :],
                    w.at[pl.ds(row, piece), pl.ds(col, HID)],
                    sem.at[i],
                )
                copy.start()
                loads[-1].append(copy)
    return loads


def load_rows(ny, y_ref, sources, rows, sem):
    own = sources[0]
    block, half = own.shape[0], sources[3].shape[0]
    loads = []
    for n, (ahead, skip) in enumerate(((0, 0), (ny - 1, 0), (1, 0), (2, 0), (2, half))):
        at = pl.multiple_of(lax.rem(y_ref[0] + ahead, ny) * block + skip, half)
        source = sources[n]
        loads.append(pltpu.make_async_copy(source, rows.at[pl.ds(at, source.shape[0]), :], sem.at[n]))
        loads[-1].start()
    return loads


def pre_kernel(nz, nx, ny, y_ref, s0, s1, s2, s3, s4, w_hbm, gu_ref, tok, w, row_sem, w_sem):
    features = tok.shape[1]
    chunk = features // nx
    rows = load_rows(ny, y_ref, (s0, s1, s2, s3, s4), tok, row_sem)
    loads = load_weights(nz, nx, features, w_hbm, w, w_sem, (0, 1))
    for copy in rows:
        copy.wait()
    for x in range(nx):
        for copy in loads[x]:
            copy.wait()
        span = slice(x * chunk, (x + 1) * chunk)
        gu = dot(tok[:, span], w[span, :], ((1,), (0,)))
        if x == 0:
            gu_ref[...] = gu
        else:
            gu_ref[...] += gu


def load_halves(low_hbm, high_hbm, ext, sem):
    cut = low_hbm.shape[1]
    loads = [
        pltpu.make_async_copy(low_hbm, ext.at[:, pl.ds(0, cut)], sem.at[5]),
        pltpu.make_async_copy(high_hbm, ext.at[:, pl.ds(cut, high_hbm.shape[1])], sem.at[6]),
    ]
    for copy in loads:
        copy.start()
    return loads


def prob_of(ext, features):
    extra = ext[:, features:].astype(F32)
    return extra[:, 0:1] + extra[:, 1:2]


def expert_kernel(nz, nx, low_hbm, high_hbm, w_hbm, gu_ref, part_hbm, grad_ref, hidden_ref,
                  ext, w, part, d_acc, row_sem, w_sem, part_sem):
    features = w.shape[0]
    chunk = features // nx
    cut = low_hbm.shape[1]
    wide = nz * HID
    load_low, load_high = load_halves(low_hbm, high_hbm, ext, row_sem)
    loads_d = load_weights(nz, nx, features, w_hbm, w, w_sem, (2,))
    loads = load_weights(nz, nx, features, w_hbm, w, w_sem, (0, 1))
    load_low.wait()
    high_in = False
    for x in range(nx):
        if (x + 1) * chunk > cut and not high_in:
            load_high.wait()
            high_in = True
        for copy in loads_d[x]:
            copy.wait()
        span = slice(x * chunk, (x + 1) * chunk)
        dg = dot(ext[:, span], w[span, 2 * wide :], ((1,), (0,)))
        if x == 0:
            d_acc[...] = dg
        else:
            d_acc[...] += dg
    prob = prob_of(ext, features)
    gate_pre, up_pre = gu_ref[:, :wide], gu_ref[:, wide:]
    down_grad = d_acc[...]
    sig = jax.nn.sigmoid(gate_pre)
    act = gate_pre * sig
    hidden = (act * up_pre).astype(BF16)
    hidden_ref[...] = hidden
    scores = jnp.sum(hidden.astype(F32) * down_grad, axis=1, keepdims=True)
    hidden_grad = prob * down_grad
    grad_ref[:, :wide] = (hidden_grad * up_pre * sig * (1.0 + gate_pre * (1.0 - sig))).astype(BF16)
    grad_ref[:, wide:] = (hidden_grad * act).astype(BF16)
    gu_grad = grad_ref[...]
    lane = lax.broadcasted_iota(jnp.int32, (scores.shape[0], PAD), 1)
    high = scores.astype(BF16).astype(F32)
    low = scores - high
    part[:, features:] = jnp.where(lane == 0, high, jnp.where(lane == 1, low, 0.0)).astype(BF16)
    stores = []
    for x in range(nx):
        for copy in loads[x]:
            copy.wait()
        span = slice(x * chunk, (x + 1) * chunk)
        part[:, span] = dot(gu_grad, w[span, : 2 * wide], ((1,), (1,))).astype(BF16)
        if x == nx - 1:
            span = slice(x * chunk, features + PAD)
        copy = pltpu.make_async_copy(part.at[:, span], part_hbm.at[:, span], part_sem.at[x])
        copy.start()
        stores.append(copy)
    for copy in stores:
        copy.wait()


def terms_kernel(nz, nx, ny, y_ref, s0, s1, s2, s3, s4, low_hbm, high_hbm, grad_ref, hidden_ref, terms_hbm,
                 tok, ext, terms, row_sem, terms_sem):
    features = tok.shape[1]
    chunk = features // nx
    piece = chunk // 2
    wide = nz * HID
    rows = load_rows(ny, y_ref, (s0, s1, s2, s3, s4), tok, row_sem)
    rows += load_halves(low_hbm, high_hbm, ext, row_sem)
    for copy in rows:
        copy.wait()
    prob = prob_of(ext, features)
    gu_grad, hidden = grad_ref[...], hidden_ref[...]
    stores = []
    for x in range(nx):
        span = slice(x * chunk, (x + 1) * chunk)
        terms[span, : 2 * wide] = dot(tok[:, span], gu_grad, ((0,), (0,))).astype(BF16)
        scaled = (prob * ext[:, span].astype(F32)).astype(BF16)
        terms[span, 2 * wide :] = dot(scaled, hidden, ((0,), (0,))).astype(BF16)
        for m, i, row, col in pieces(nz, nx, x, features):
            copy = pltpu.make_async_copy(
                terms.at[pl.ds(row, piece), pl.ds(col, HID)],
                terms_hbm.at[pl.ds(i * piece, piece), :],
                terms_sem.at[i],
            )
            copy.start()
            stores.append(copy)
    for copy in stores:
        copy.wait()


ANYWHERE = pl.BlockSpec(memory_space=pl.ANY)
SCALAR = pl.BlockSpec(memory_space=pltpu.SMEM)
INSIDE = pl.BlockSpec(memory_space=pltpu.VMEM)


def pre_math(y, tok, w, rows, nz, nx):
    features = tok[0].shape[1]
    wide = nz * HID
    count = nz * nx * 2 * KINDS
    return pl.pallas_call(
        functools.partial(pre_kernel, nz, nx, rows // tok[0].shape[0]),
        name="pre_math",
        out_shape=jax.ShapeDtypeStruct((rows, 2 * wide), F32),
        in_specs=[SCALAR] + [ANYWHERE] * (len(tok) + 1),
        out_specs=INSIDE,
        scratch_shapes=[
            pltpu.VMEM((rows, features), BF16),
            pltpu.VMEM((features, 2 * wide), BF16),
            pltpu.SemaphoreType.DMA((5,)),
            pltpu.SemaphoreType.DMA((count,)),
        ],
        cost_estimate=pl.CostEstimate(
            flops=4 * rows * features * wide,
            transcendentals=0,
            bytes_accessed=2 * features * (2 * wide + rows),
        ),
    )(y, *tok, w)


def expert_math(low, high, w, gu, nz, nx):
    rows, features = gu.shape[0], low.shape[1] + high.shape[1] - PAD
    wide = nz * HID
    count = nz * nx * 2 * KINDS
    return pl.pallas_call(
        functools.partial(expert_kernel, nz, nx),
        name="expert_math",
        out_shape=(
            jax.ShapeDtypeStruct((rows, features + PAD), BF16),
            jax.ShapeDtypeStruct((rows, 2 * wide), BF16),
            jax.ShapeDtypeStruct((rows, wide), BF16),
        ),
        in_specs=[ANYWHERE] * 3 + [INSIDE],
        out_specs=(ANYWHERE, INSIDE, INSIDE),
        scratch_shapes=[
            pltpu.VMEM((rows, features + PAD), BF16),
            pltpu.VMEM((features, KINDS * wide), BF16),
            pltpu.VMEM((rows, features + PAD), BF16),
            pltpu.VMEM((rows, wide), F32),
            pltpu.SemaphoreType.DMA((7,)),
            pltpu.SemaphoreType.DMA((count,)),
            pltpu.SemaphoreType.DMA((nx,)),
        ],
        cost_estimate=pl.CostEstimate(
            flops=6 * rows * features * wide,
            transcendentals=rows * wide,
            bytes_accessed=2 * features * (KINDS * wide + 2 * rows),
        ),
    )(low, high, w, gu)


def terms_math(y, tok, low, high, grad, hidden, held, nz, nx):
    rows, features = low.shape[0], tok[0].shape[1]
    wide = nz * HID
    count = nz * nx * 2 * KINDS
    return pl.pallas_call(
        functools.partial(terms_kernel, nz, nx, rows // tok[0].shape[0]),
        name="terms_math",
        out_shape=jax.ShapeDtypeStruct((held, HID), BF16),
        in_specs=[SCALAR] + [ANYWHERE] * (len(tok) + 2) + [INSIDE] * 2,
        out_specs=ANYWHERE,
        scratch_shapes=[
            pltpu.VMEM((rows, features), BF16),
            pltpu.VMEM((rows, features + PAD), BF16),
            pltpu.VMEM((features, KINDS * wide), BF16),
            pltpu.SemaphoreType.DMA((7,)),
            pltpu.SemaphoreType.DMA((count,)),
        ],
        cost_estimate=pl.CostEstimate(
            flops=6 * rows * features * wide,
            transcendentals=0,
            bytes_accessed=2 * features * (KINDS * wide + 2 * rows),
        ),
    )(y, *tok, low, high, grad, hidden)


def layer(tokens, grad_out, routes, route_probs, gate_weight, up_weight, down_weight):
    count, features = tokens.shape
    experts, ny = lax.axis_size("e"), lax.axis_size("y")
    nz, nx = lax.axis_size("zp"), lax.axis_size("x")
    slots = experts * CAP

    stored = jnp.concatenate([gate_weight[0], up_weight[0], down_weight[0]], axis=0)
    paired = lax.ppermute(stored, "zp", SWAP)
    weights = lax.all_gather(jnp.concatenate([stored, paired], axis=0), HOLD, axis=0, tiled=True)

    ids = jnp.arange(experts, dtype=jnp.int32)
    first, second = routes[:, 0:1] == ids, routes[:, 1:2] == ids
    named = (first | second).astype(BF16)
    place = jnp.arange(count)
    before = (place[:, None] > place[None, :]).astype(BF16)
    rank = dot(before, named, ((1,), (0,))).T
    taken = (named.T[:, None, :] > 0) & (rank[:, None, :] == jnp.arange(CAP, dtype=F32)[None, :, None])
    prob = jnp.where(first, route_probs[:, 0:1], 0.0) + jnp.where(second, route_probs[:, 1:2], 0.0)
    slot_prob = jnp.sum(jnp.where(taken, prob.T[:, None, :], 0.0), axis=2).reshape(slots)
    select = taken.astype(BF16).reshape(slots, count)
    send_tok = dot(select, tokens, ((1,), (0,))).astype(BF16)
    send_grd = dot(select, grad_out, ((1,), (0,))).astype(BF16)
    send_grd = jnp.concatenate([send_grd, columns(slot_prob)], axis=1)

    own = swapped(send_tok, "e")
    own, send_grd = lax.optimization_barrier((own, send_grd))
    up, down = [(i, (i + 1) % ny) for i in range(ny)], [(i, (i - 1) % ny) for i in range(ny)]
    half = slots // 2
    left, right = lax.ppermute(own, "y", up), lax.ppermute(own, "y", down)
    halves = left[:half], right[half:]
    far = lax.ppermute(halves[0], "y", up), lax.ppermute(halves[1], "y", down)
    came_grd = swapped(send_grd, "e")
    cut = features // 2
    rows_high = lax.all_gather(came_grd[:, cut:], "y", axis=0, tiled=True)
    rows_low = shared(came_grd[:, :cut], "y")

    y = lax.axis_index("y").astype(jnp.int32).reshape(1)
    tok = (own, left, right) + far
    gate_up = pre_math(y, tok, weights, ny * slots, nz, nx)
    part, grad, hidden = expert_math(rows_low, rows_high, weights, gate_up, nz, nx)
    back = swapped(part, "y")
    terms = terms_math(y, tok, rows_low, rows_high, grad, hidden, weights.shape[0], nz, nx)
    sums = lax.psum_scatter(terms, HOLD, scatter_dimension=0, tiled=True)
    kept, given = jnp.split(sums, 2, axis=0)
    given = lax.ppermute(given, "zp", SWAP)
    grads = (kept.astype(F32) + given.astype(F32)).astype(BF16).reshape(KINDS, 1, -1, HID)

    back = jnp.sum(back.astype(F32).reshape(ny, slots, -1), axis=0)
    back_score = columns(joined(back[:, features : features + 2]))
    back = jnp.concatenate([back[:, :features].astype(BF16), back_score], axis=1)
    back = swapped(back, "e")
    grad_tokens = dot(select, back[:, :features], ((0,), (0,))).astype(BF16)
    score = joined(back[:, features : features + 2]).reshape(experts, CAP, 1)
    score = jnp.sum(jnp.where(taken, score, 0.0), axis=1).T
    grad_probs = jnp.stack(
        [jnp.sum(jnp.where(first, score, 0.0), axis=1), jnp.sum(jnp.where(second, score, 0.0), axis=1)], axis=1
    )
    return (grad_tokens, grad_probs, grads[0], grads[1], grads[2])


def solution(mesh):
    fine = Mesh(mesh.devices.reshape(mesh.shape["ep"] // GROUP, 2, GROUP // 2, -1, 2), AXES)
    rows, stored = P(AXES, None), P(AXES[:3], AXES[3:], None)
    return jax.shard_map(
        layer,
        mesh=fine,
        in_specs=(rows, rows, rows, rows, stored, stored, stored),
        out_specs=(rows, rows, stored, stored, stored),
        check_vma=False,
    )
```

```python
import functools

import jax
import jax.numpy as jnp
from jax import lax
from jax.experimental import pallas as pl
from jax.experimental.pallas import tpu as pltpu
from jax.sharding import Mesh, PartitionSpec as P


GROUP = 8
CAP = 8
HID = 128
PAD = 128
F32 = jnp.float32
BF16 = jnp.bfloat16
AXES = ("e", "zp", "y", "x", "c")
HOLD = ("x", "c")
SWAP = [(0, 1), (1, 0)]
KINDS = 3
PRE_GRANT = 20 << 20
EXPERT_GRANT = 58 << 20


def dot(a, b, dims):
    return lax.dot_general(a, b, (dims, ((), ())), preferred_element_type=F32)


def split(v):
    high = lax.reduce_precision(v, 8, 7)
    return high.astype(BF16), (v - high).astype(BF16)


def columns(v):
    high, low = split(v)
    blank = jnp.zeros((v.shape[0], PAD - 2), BF16)
    return jnp.concatenate([high[:, None], low[:, None], blank], axis=1)


def joined(cols):
    return cols[:, 0].astype(F32) + cols[:, 1].astype(F32)


def swapped(x, axis):
    return lax.all_to_all(x, axis, 0, 0, tiled=True)


def shared(x, axis):
    n = lax.axis_size(axis)
    return swapped(jnp.broadcast_to(x[None], (n,) + x.shape).reshape(n * x.shape[0], -1), axis)


def pieces(nz, nx, x, features):
    chunk = features // nx
    piece = chunk // 2
    for c in range(2):
        for z in range(nz):
            for m in range(KINDS):
                yield m, ((x * 2 + c) * nz + z) * KINDS + m, x * chunk + c * piece, (m * nz + z) * HID


def load_weights(nz, nx, features, w_hbm, w, sem, kinds):
    piece = features // nx // 2
    loads = []
    for x in range(nx):
        loads.append([])
        for m, i, row, col in pieces(nz, nx, x, features):
            if m in kinds:
                copy = pltpu.make_async_copy(
                    w_hbm.at[pl.ds(i * piece, piece), :],
                    w.at[pl.ds(row, piece), pl.ds(col, HID)],
                    sem.at[i],
                )
                copy.start()
                loads[-1].append(copy)
    return loads


def pre_kernel(nz, nx, ny, y_ref, s0, s1, s2, s3, s4, w_hbm, rows, w, gu_ref, w_sem):
    features = rows.shape[1]
    chunk = features // nx
    wide = nz * HID
    loads = load_weights(nz, nx, features, w_hbm, w, w_sem, range(KINDS))
    block, half = s0.shape[0], s3.shape[0]
    for source, ahead, skip in ((s0, 0, 0), (s1, ny - 1, 0), (s2, 1, 0), (s3, 2, 0), (s4, 2, half)):
        at = pl.multiple_of(lax.rem(y_ref[0] + ahead, ny) * block + skip, half)
        rows[pl.ds(at, source.shape[0]), :] = source[...]
    for x in range(nx):
        for copy in loads[x]:
            copy.wait()
        span = slice(x * chunk, (x + 1) * chunk)
        gu = dot(rows[:, span], w[span, : 2 * wide], ((1,), (0,)))
        if x == 0:
            gu_ref[...] = gu
        else:
            gu_ref[...] += gu


def expert_kernel(nz, nx, rows_hbm, ext, w_hbm, gu_hbm, terms_hbm, part, rows, w, gu_ref, terms, in_sem, terms_sem):
    features = w.shape[0]
    chunk = features // nx
    piece = chunk // 2
    wide = nz * HID
    down = pl.ds(2 * wide, wide)
    load_d = pltpu.make_async_copy(w_hbm.at[:, down], w.at[:, down], in_sem.at[0])
    load_gu = pltpu.make_async_copy(gu_hbm, gu_ref, in_sem.at[1])
    loads = [load_d, load_gu]
    for x in range(nx):
        span = pl.ds(x * chunk, chunk)
        loads.append(pltpu.make_async_copy(rows_hbm.at[:, span], rows.at[:, span], in_sem.at[2 + x]))
    for x in range(nx):
        span, cols = pl.ds(x * chunk, chunk), pl.ds(0, 2 * wide)
        loads.append(pltpu.make_async_copy(w_hbm.at[span, cols], w.at[span, cols], in_sem.at[2 + nx + x]))
    for copy in loads:
        copy.start()
    load_d.wait()
    down_grad = dot(ext[:, :features], w[:, 2 * wide :], ((1,), (0,)))
    extra = ext[:, features:].astype(F32)
    prob = extra[:, 0:1] + extra[:, 1:2]
    load_gu.wait()
    gate_pre, up_pre = gu_ref[:, :wide], gu_ref[:, wide:]
    sig = jax.nn.sigmoid(gate_pre)
    act = gate_pre * sig
    hidden = (act * up_pre).astype(BF16)
    scores = jnp.sum(hidden.astype(F32) * down_grad, axis=1, keepdims=True)
    hidden_grad = prob * down_grad
    gate_grad = (hidden_grad * up_pre * sig * (1.0 + gate_pre * (1.0 - sig))).astype(BF16)
    up_grad = (hidden_grad * act).astype(BF16)
    gu_grad = jnp.concatenate([gate_grad, up_grad], axis=1)
    stores = []
    for x in range(nx):
        loads[2 + x].wait()
        span = slice(x * chunk, (x + 1) * chunk)
        terms[span, : 2 * wide] = dot(rows[:, span], gu_grad, ((0,), (0,))).astype(BF16)
        scaled = (prob * ext[:, span].astype(F32)).astype(BF16)
        terms[span, 2 * wide :] = dot(scaled, hidden, ((0,), (0,))).astype(BF16)
        for m, i, row, col in pieces(nz, nx, x, features):
            copy = pltpu.make_async_copy(
                terms.at[pl.ds(row, piece), pl.ds(col, HID)],
                terms_hbm.at[pl.ds(i * piece, piece), :],
                terms_sem.at[i],
            )
            copy.start()
            stores.append(copy)
    lane = lax.broadcasted_iota(jnp.int32, (scores.shape[0], PAD), 1)
    high = scores.astype(BF16).astype(F32)
    low = scores - high
    part[:, features:] = jnp.where(lane == 0, high, jnp.where(lane == 1, low, 0.0)).astype(BF16)
    for x in range(nx):
        loads[2 + nx + x].wait()
        span = slice(x * chunk, (x + 1) * chunk)
        part[:, span] = dot(gu_grad, w[span, : 2 * wide], ((1,), (1,))).astype(BF16)
    for copy in stores:
        copy.wait()


ANYWHERE = pl.BlockSpec(memory_space=pl.ANY)
SCALAR = pl.BlockSpec(memory_space=pltpu.SMEM)
INSIDE = pl.BlockSpec(memory_space=pltpu.VMEM)


def pre_math(y, tok, w, nrows, nz, nx):
    features = tok[0].shape[1]
    wide = nz * HID
    return pl.pallas_call(
        functools.partial(pre_kernel, nz, nx, nrows // tok[0].shape[0]),
        name="pre_math",
        out_shape=(
            jax.ShapeDtypeStruct((nrows, features), BF16),
            jax.ShapeDtypeStruct((features, KINDS * wide), BF16),
            jax.ShapeDtypeStruct((nrows, 2 * wide), F32),
        ),
        in_specs=[SCALAR] + [INSIDE] * len(tok) + [ANYWHERE],
        out_specs=(INSIDE,) * 3,
        scratch_shapes=[pltpu.SemaphoreType.DMA((nz * nx * 2 * KINDS,))],
        compiler_params=pltpu.CompilerParams(vmem_limit_bytes=PRE_GRANT),
        cost_estimate=pl.CostEstimate(
            flops=4 * nrows * features * wide,
            transcendentals=0,
            bytes_accessed=2 * features * (KINDS * wide + nrows),
        ),
    )(y, *tok, w)


def expert_math(rows, ext, w, gu, held, nz, nx):
    count, features = rows.shape
    wide = nz * HID
    copies = nz * nx * 2 * KINDS
    return pl.pallas_call(
        functools.partial(expert_kernel, nz, nx),
        name="expert_math",
        out_shape=(
            pltpu.HBM((held, HID), BF16),
            jax.ShapeDtypeStruct((count, features + PAD), BF16),
        ),
        in_specs=[ANYWHERE, INSIDE, ANYWHERE, ANYWHERE],
        out_specs=(ANYWHERE, INSIDE),
        scratch_shapes=[
            pltpu.VMEM((count, features), BF16),
            pltpu.VMEM((features, KINDS * wide), BF16),
            pltpu.VMEM((count, 2 * wide), F32),
            pltpu.VMEM((features, KINDS * wide), BF16),
            pltpu.SemaphoreType.DMA((2 + 2 * nx,)),
            pltpu.SemaphoreType.DMA((copies,)),
        ],
        compiler_params=pltpu.CompilerParams(vmem_limit_bytes=EXPERT_GRANT),
        cost_estimate=pl.CostEstimate(
            flops=12 * count * features * wide,
            transcendentals=count * wide,
            bytes_accessed=2 * features * (KINDS * wide + 2 * count),
        ),
    )(rows, ext, w, gu)


def layer(tokens, grad_out, routes, route_probs, gate_weight, up_weight, down_weight):
    count, features = tokens.shape
    experts, ny = lax.axis_size("e"), lax.axis_size("y")
    nz, nx = lax.axis_size("zp"), lax.axis_size("x")
    slots = experts * CAP

    stored = jnp.concatenate([gate_weight[0], up_weight[0], down_weight[0]], axis=0)
    paired = lax.ppermute(stored, "zp", SWAP)
    weights = lax.all_gather(jnp.concatenate([stored, paired], axis=0), HOLD, axis=0, tiled=True)

    ids = jnp.arange(experts, dtype=jnp.int32)
    first, second = routes[:, 0:1] == ids, routes[:, 1:2] == ids
    named = (first | second).astype(BF16)
    place = jnp.arange(count)
    before = (place[:, None] > place[None, :]).astype(BF16)
    rank = dot(before, named, ((1,), (0,))).T
    taken = (named.T[:, None, :] > 0) & (rank[:, None, :] == jnp.arange(CAP, dtype=F32)[None, :, None])
    prob = jnp.where(first, route_probs[:, 0:1], 0.0) + jnp.where(second, route_probs[:, 1:2], 0.0)
    slot_prob = jnp.sum(jnp.where(taken, prob.T[:, None, :], 0.0), axis=2).reshape(slots)
    select = taken.astype(BF16).reshape(slots, count)
    send_tok = dot(select, tokens, ((1,), (0,))).astype(BF16)
    send_grd = dot(select, grad_out, ((1,), (0,))).astype(BF16)
    send_grd = jnp.concatenate([send_grd, columns(slot_prob)], axis=1)

    own = swapped(send_tok, "e")
    own, send_grd = lax.optimization_barrier((own, send_grd))
    up, down = [(i, (i + 1) % ny) for i in range(ny)], [(i, (i - 1) % ny) for i in range(ny)]
    half = slots // 2
    left, right = lax.ppermute(own, "y", up), lax.ppermute(own, "y", down)
    halves = left[:half], right[half:]
    far = lax.ppermute(halves[0], "y", up), lax.ppermute(halves[1], "y", down)
    came_grd = swapped(send_grd, "e")
    rows_ext = shared(came_grd, "y")

    y = lax.axis_index("y").astype(jnp.int32).reshape(1)
    rows, blocks, gate_up = pre_math(y, (own, left, right) + far, weights, ny * slots, nz, nx)
    terms, part = expert_math(rows, rows_ext, blocks, gate_up, weights.shape[0], nz, nx)
    back = swapped(part, "y")
    sums = lax.psum_scatter(terms, HOLD, scatter_dimension=0, tiled=True)
    kept, given = jnp.split(sums, 2, axis=0)
    given = lax.ppermute(given, "zp", SWAP)
    grads = (kept.astype(F32) + given.astype(F32)).astype(BF16).reshape(KINDS, 1, -1, HID)

    back = jnp.sum(back.astype(F32).reshape(ny, slots, -1), axis=0)
    back_score = columns(joined(back[:, features : features + 2]))
    back = jnp.concatenate([back[:, :features].astype(BF16), back_score], axis=1)
    back = swapped(back, "e")
    grad_tokens = dot(select, back[:, :features], ((0,), (0,))).astype(BF16)
    score = joined(back[:, features : features + 2]).reshape(experts, CAP, 1)
    score = jnp.sum(jnp.where(taken, score, 0.0), axis=1).T
    grad_probs = jnp.stack(
        [jnp.sum(jnp.where(first, score, 0.0), axis=1), jnp.sum(jnp.where(second, score, 0.0), axis=1)], axis=1
    )
    return (grad_tokens, grad_probs, grads[0], grads[1], grads[2])


def solution(mesh):
    fine = Mesh(mesh.devices.reshape(mesh.shape["ep"] // GROUP, 2, GROUP // 2, -1, 2), AXES)
    rows, stored = P(AXES, None), P(AXES[:3], AXES[3:], None)
    return jax.shard_map(
        layer,
        mesh=fine,
        in_specs=(rows, rows, rows, rows, stored, stored, stored),
        out_specs=(rows, rows, stored, stored, stored),
        check_vma=False,
    )
```

```python
import functools

import jax
import jax.numpy as jnp
from jax import lax
from jax.experimental import pallas as pl
from jax.experimental.pallas import tpu as pltpu
from jax.sharding import Mesh, PartitionSpec as P


GROUP = 8
CAP = 8
HID = 128
PAD = 128
F32 = jnp.float32
BF16 = jnp.bfloat16
AXES = ("e", "zp", "y", "x", "c")
HOLD = ("x", "c")
SWAP = [(0, 1), (1, 0)]
KINDS = 3
PRE_GRANT = 20 << 20
EXPERT_GRANT = 58 << 20


def dot(a, b, dims):
    return lax.dot_general(a, b, (dims, ((), ())), preferred_element_type=F32)


def split(v):
    high = lax.reduce_precision(v, 8, 7)
    return high.astype(BF16), (v - high).astype(BF16)


def columns(v):
    high, low = split(v)
    blank = jnp.zeros((v.shape[0], PAD - 2), BF16)
    return jnp.concatenate([high[:, None], low[:, None], blank], axis=1)


def joined(cols):
    return cols[:, 0].astype(F32) + cols[:, 1].astype(F32)


def swapped(x, axis):
    return lax.all_to_all(x, axis, 0, 0, tiled=True)


def shared(x, axis):
    n = lax.axis_size(axis)
    return swapped(jnp.broadcast_to(x[None], (n,) + x.shape).reshape(n * x.shape[0], -1), axis)


def pieces(nz, nx, x, features):
    chunk = features // nx
    piece = chunk // 2
    for c in range(2):
        for z in range(nz):
            for m in range(KINDS):
                yield m, ((x * 2 + c) * nz + z) * KINDS + m, x * chunk + c * piece, (m * nz + z) * HID


def load_weights(nz, nx, features, w_hbm, w, sem, kinds):
    piece = features // nx // 2
    loads = []
    for x in range(nx):
        loads.append([])
        for m, i, row, col in pieces(nz, nx, x, features):
            if m in kinds:
                copy = pltpu.make_async_copy(
                    w_hbm.at[pl.ds(i * piece, piece), :],
                    w.at[pl.ds(row, piece), pl.ds(col, HID)],
                    sem.at[i],
                )
                copy.start()
                loads[-1].append(copy)
    return loads


def pre_kernel(nz, nx, ny, y_ref, s0, s1, s2, s3, s4, w_hbm, rows, w, gu_ref, w_sem):
    features = rows.shape[1]
    chunk = features // nx
    wide = nz * HID
    loads = load_weights(nz, nx, features, w_hbm, w, w_sem, range(KINDS))
    block, half = s0.shape[0], s3.shape[0]
    for source, ahead, skip in ((s0, 0, 0), (s1, ny - 1, 0), (s2, 1, 0), (s3, 2, 0), (s4, 2, half)):
        at = pl.multiple_of(lax.rem(y_ref[0] + ahead, ny) * block + skip, half)
        rows[pl.ds(at, source.shape[0]), :] = source[...]
    for x in range(nx):
        for copy in loads[x]:
            copy.wait()
        span = slice(x * chunk, (x + 1) * chunk)
        gu = dot(rows[:, span], w[span, : 2 * wide], ((1,), (0,)))
        if x == 0:
            gu_ref[...] = gu
        else:
            gu_ref[...] += gu


def expert_kernel(nz, nx, rows_hbm, ext_hbm, w_hbm, gu_hbm, terms_hbm, part_hbm,
                  rows, ext, w, gu_ref, terms, part, in_sem, terms_sem, part_sem):
    features = w.shape[0]
    chunk = features // nx
    piece = chunk // 2
    wide = nz * HID
    down, cols = pl.ds(2 * wide, wide), pl.ds(0, 2 * wide)
    spans = [pl.ds(x * chunk, chunk) for x in range(nx)]
    tail = pl.ds(features, PAD)
    moves = [(w_hbm.at[span, down], w.at[span, down]) for span in spans]
    moves += [(ext_hbm.at[:, span], ext.at[:, span]) for span in spans]
    moves += [(rows_hbm.at[:, span], rows.at[:, span]) for span in spans]
    moves += [(w_hbm.at[span, cols], w.at[span, cols]) for span in spans]
    moves += [(ext_hbm.at[:, tail], ext.at[:, tail]), (gu_hbm, gu_ref)]
    loads = [pltpu.make_async_copy(source, target, in_sem.at[n]) for n, (source, target) in enumerate(moves)]
    load_extra, load_gu = loads[4 * nx :]
    for x in range(nx):
        loads[x].start()
        loads[nx + x].start()
    load_extra.start()
    load_gu.start()
    for copy in loads[2 * nx : 4 * nx]:
        copy.start()
    down_grad = None
    for x in range(nx):
        loads[x].wait()
        loads[nx + x].wait()
        span = slice(x * chunk, (x + 1) * chunk)
        term = dot(ext[:, span], w[span, 2 * wide :], ((1,), (0,)))
        down_grad = term if x == 0 else down_grad + term
    load_extra.wait()
    extra = ext[:, features:].astype(F32)
    prob = extra[:, 0:1] + extra[:, 1:2]
    load_gu.wait()
    gate_pre, up_pre = gu_ref[:, :wide], gu_ref[:, wide:]
    sig = jax.nn.sigmoid(gate_pre)
    act = gate_pre * sig
    hidden = (act * up_pre).astype(BF16)
    scores = jnp.sum(hidden.astype(F32) * down_grad, axis=1, keepdims=True)
    hidden_grad = prob * down_grad
    gate_grad = (hidden_grad * up_pre * sig * (1.0 + gate_pre * (1.0 - sig))).astype(BF16)
    up_grad = (hidden_grad * act).astype(BF16)
    gu_grad = jnp.concatenate([gate_grad, up_grad], axis=1)
    stores = []
    for x in range(nx):
        loads[2 * nx + x].wait()
        span = slice(x * chunk, (x + 1) * chunk)
        terms[span, : 2 * wide] = dot(rows[:, span], gu_grad, ((0,), (0,))).astype(BF16)
        scaled = (prob * ext[:, span].astype(F32)).astype(BF16)
        terms[span, 2 * wide :] = dot(scaled, hidden, ((0,), (0,))).astype(BF16)
        for m, i, row, col in pieces(nz, nx, x, features):
            copy = pltpu.make_async_copy(
                terms.at[pl.ds(row, piece), pl.ds(col, HID)],
                terms_hbm.at[pl.ds(i * piece, piece), :],
                terms_sem.at[i],
            )
            copy.start()
            stores.append(copy)
    lane = lax.broadcasted_iota(jnp.int32, (scores.shape[0], PAD), 1)
    high = scores.astype(BF16).astype(F32)
    low = scores - high
    part[:, features:] = jnp.where(lane == 0, high, jnp.where(lane == 1, low, 0.0)).astype(BF16)
    for x in range(nx):
        loads[3 * nx + x].wait()
        span = slice(x * chunk, (x + 1) * chunk)
        part[:, span] = dot(gu_grad, w[span, : 2 * wide], ((1,), (1,))).astype(BF16)
        if x == nx - 1:
            span = slice(x * chunk, features + PAD)
        copy = pltpu.make_async_copy(part.at[:, span], part_hbm.at[:, span], part_sem.at[x])
        copy.start()
        stores.append(copy)
    for copy in stores:
        copy.wait()


ANYWHERE = pl.BlockSpec(memory_space=pl.ANY)
SCALAR = pl.BlockSpec(memory_space=pltpu.SMEM)
INSIDE = pl.BlockSpec(memory_space=pltpu.VMEM)


def pre_math(y, tok, w, nrows, nz, nx):
    features = tok[0].shape[1]
    wide = nz * HID
    return pl.pallas_call(
        functools.partial(pre_kernel, nz, nx, nrows // tok[0].shape[0]),
        name="pre_math",
        out_shape=(
            jax.ShapeDtypeStruct((nrows, features), BF16),
            jax.ShapeDtypeStruct((features, KINDS * wide), BF16),
            jax.ShapeDtypeStruct((nrows, 2 * wide), F32),
        ),
        in_specs=[SCALAR] + [INSIDE] * len(tok) + [ANYWHERE],
        out_specs=(INSIDE,) * 3,
        scratch_shapes=[pltpu.SemaphoreType.DMA((nz * nx * 2 * KINDS,))],
        compiler_params=pltpu.CompilerParams(vmem_limit_bytes=PRE_GRANT),
        cost_estimate=pl.CostEstimate(
            flops=4 * nrows * features * wide,
            transcendentals=0,
            bytes_accessed=2 * features * (KINDS * wide + nrows),
        ),
    )(y, *tok, w)


def expert_math(rows, ext, w, gu, held, nz, nx):
    count, features = rows.shape
    wide = nz * HID
    copies = nz * nx * 2 * KINDS
    return pl.pallas_call(
        functools.partial(expert_kernel, nz, nx),
        name="expert_math",
        out_shape=(
            pltpu.HBM((held, HID), BF16),
            jax.ShapeDtypeStruct((count, features + PAD), BF16),
        ),
        in_specs=[ANYWHERE] * 4,
        out_specs=(ANYWHERE, ANYWHERE),
        scratch_shapes=[
            pltpu.VMEM((count, features), BF16),
            pltpu.VMEM((count, features + PAD), BF16),
            pltpu.VMEM((features, KINDS * wide), BF16),
            pltpu.VMEM((count, 2 * wide), F32),
            pltpu.VMEM((features, KINDS * wide), BF16),
            pltpu.VMEM((count, features + PAD), BF16),
            pltpu.SemaphoreType.DMA((2 + 4 * nx,)),
            pltpu.SemaphoreType.DMA((copies,)),
            pltpu.SemaphoreType.DMA((nx,)),
        ],
        compiler_params=pltpu.CompilerParams(vmem_limit_bytes=EXPERT_GRANT),
        cost_estimate=pl.CostEstimate(
            flops=12 * count * features * wide,
            transcendentals=count * wide,
            bytes_accessed=2 * features * (KINDS * wide + 2 * count),
        ),
    )(rows, ext, w, gu)


def layer(tokens, grad_out, routes, route_probs, gate_weight, up_weight, down_weight):
    count, features = tokens.shape
    experts, ny = lax.axis_size("e"), lax.axis_size("y")
    nz, nx = lax.axis_size("zp"), lax.axis_size("x")
    slots = experts * CAP

    stored = jnp.concatenate([gate_weight[0], up_weight[0], down_weight[0]], axis=0)
    paired = lax.ppermute(stored, "zp", SWAP)
    weights = lax.all_gather(jnp.concatenate([stored, paired], axis=0), HOLD, axis=0, tiled=True)

    ids = jnp.arange(experts, dtype=jnp.int32)
    first, second = routes[:, 0:1] == ids, routes[:, 1:2] == ids
    named = (first | second).astype(BF16)
    place = jnp.arange(count)
    before = (place[:, None] > place[None, :]).astype(BF16)
    rank = dot(before, named, ((1,), (0,))).T
    taken = (named.T[:, None, :] > 0) & (rank[:, None, :] == jnp.arange(CAP, dtype=F32)[None, :, None])
    prob = jnp.where(first, route_probs[:, 0:1], 0.0) + jnp.where(second, route_probs[:, 1:2], 0.0)
    slot_prob = jnp.sum(jnp.where(taken, prob.T[:, None, :], 0.0), axis=2).reshape(slots)
    select = taken.astype(BF16).reshape(slots, count)
    send_tok = dot(select, tokens, ((1,), (0,))).astype(BF16)
    send_grd = dot(select, grad_out, ((1,), (0,))).astype(BF16)
    send_grd = jnp.concatenate([send_grd, columns(slot_prob)], axis=1)

    own = swapped(send_tok, "e")
    own, send_grd = lax.optimization_barrier((own, send_grd))
    up, down = [(i, (i + 1) % ny) for i in range(ny)], [(i, (i - 1) % ny) for i in range(ny)]
    half = slots // 2
    left, right = lax.ppermute(own, "y", up), lax.ppermute(own, "y", down)
    halves = left[:half], right[half:]
    far = lax.ppermute(halves[0], "y", up), lax.ppermute(halves[1], "y", down)
    came_grd = swapped(send_grd, "e")
    rows_ext = shared(came_grd, "y")

    y = lax.axis_index("y").astype(jnp.int32).reshape(1)
    rows, blocks, gate_up = pre_math(y, (own, left, right) + far, weights, ny * slots, nz, nx)
    terms, part = expert_math(rows, rows_ext, blocks, gate_up, weights.shape[0], nz, nx)
    back = swapped(part, "y")
    sums = lax.psum_scatter(terms, HOLD, scatter_dimension=0, tiled=True)
    kept, given = jnp.split(sums, 2, axis=0)
    given = lax.ppermute(given, "zp", SWAP)
    kept, given = kept.reshape(KINDS, 1, -1, HID), given.reshape(KINDS, 1, -1, HID)
    grads = [(kept[m].astype(F32) + given[m].astype(F32)).astype(BF16) for m in range(KINDS)]

    back = jnp.sum(back.astype(F32).reshape(ny, slots, -1), axis=0)
    back_score = columns(joined(back[:, features : features + 2]))
    back = jnp.concatenate([back[:, :features].astype(BF16), back_score], axis=1)
    back = swapped(back, "e")
    grad_tokens = dot(select, back[:, :features], ((0,), (0,))).astype(BF16)
    score = joined(back[:, features : features + 2]).reshape(experts, CAP, 1)
    score = jnp.sum(jnp.where(taken, score, 0.0), axis=1).T
    grad_probs = jnp.stack(
        [jnp.sum(jnp.where(first, score, 0.0), axis=1), jnp.sum(jnp.where(second, score, 0.0), axis=1)], axis=1
    )
    return (grad_tokens, grad_probs, grads[0], grads[1], grads[2])


def solution(mesh):
    fine = Mesh(mesh.devices.reshape(mesh.shape["ep"] // GROUP, 2, GROUP // 2, -1, 2), AXES)
    rows, stored = P(AXES, None), P(AXES[:3], AXES[3:], None)
    return jax.shard_map(
        layer,
        mesh=fine,
        in_specs=(rows, rows, rows, rows, stored, stored, stored),
        out_specs=(rows, rows, stored, stored, stored),
        check_vma=False,
    )
```

```python
import functools

import jax
import jax.numpy as jnp
from jax import lax
from jax.experimental import pallas as pl
from jax.experimental.pallas import tpu as pltpu
from jax.sharding import Mesh, PartitionSpec as P


GROUP = 8
CAP = 8
HID = 128
PAD = 128
F32 = jnp.float32
BF16 = jnp.bfloat16
AXES = ("e", "zp", "y", "x", "c")
HOLD = ("x", "c")
SWAP = [(0, 1), (1, 0)]
KINDS = 3
PRE_GRANT = 20 << 20
EXPERT_GRANT = 58 << 20


def dot(a, b, dims):
    return lax.dot_general(a, b, (dims, ((), ())), preferred_element_type=F32)


def split(v):
    high = lax.reduce_precision(v, 8, 7)
    return high.astype(BF16), (v - high).astype(BF16)


def columns(v):
    high, low = split(v)
    blank = jnp.zeros((v.shape[0], PAD - 2), BF16)
    return jnp.concatenate([high[:, None], low[:, None], blank], axis=1)


def joined(cols):
    return cols[:, 0].astype(F32) + cols[:, 1].astype(F32)


def swapped(x, axis):
    return lax.all_to_all(x, axis, 0, 0, tiled=True)


def shared(x, axis):
    n = lax.axis_size(axis)
    return swapped(jnp.broadcast_to(x[None], (n,) + x.shape).reshape(n * x.shape[0], -1), axis)


def pieces(nz, nx, x, features):
    chunk = features // nx
    piece = chunk // 2
    for c in range(2):
        for z in range(nz):
            for m in range(KINDS):
                yield m, ((x * 2 + c) * nz + z) * KINDS + m, x * chunk + c * piece, (m * nz + z) * HID


def load_weights(nz, nx, features, w_hbm, w, sem, kinds):
    piece = features // nx // 2
    loads = []
    for x in range(nx):
        loads.append([])
        for m, i, row, col in pieces(nz, nx, x, features):
            if m in kinds:
                copy = pltpu.make_async_copy(
                    w_hbm.at[pl.ds(i * piece, piece), :],
                    w.at[pl.ds(row, piece), pl.ds(col, HID)],
                    sem.at[i],
                )
                copy.start()
                loads[-1].append(copy)
    return loads


def pre_kernel(nz, nx, ny, y_ref, s0, s1, s2, s3, s4, w_hbm, rows, w, gu_ref, w_sem):
    features = rows.shape[1]
    chunk = features // nx
    wide = nz * HID
    loads = load_weights(nz, nx, features, w_hbm, w, w_sem, range(KINDS))
    block, half = s0.shape[0], s3.shape[0]
    for source, ahead, skip in ((s0, 0, 0), (s1, ny - 1, 0), (s2, 1, 0), (s3, 2, 0), (s4, 2, half)):
        at = pl.multiple_of(lax.rem(y_ref[0] + ahead, ny) * block + skip, half)
        rows[pl.ds(at, source.shape[0]), :] = source[...]
    for x in range(nx):
        for copy in loads[x]:
            copy.wait()
        span = slice(x * chunk, (x + 1) * chunk)
        gu = dot(rows[:, span], w[span, : 2 * wide], ((1,), (0,)))
        if x == 0:
            gu_ref[...] = gu
        else:
            gu_ref[...] += gu


def expert_kernel(nz, nx, rows_hbm, ext_hbm, w_hbm, gu_hbm, terms_hbm, part_hbm,
                  rows, ext, w, gu_ref, terms, part, in_sem, terms_sem, part_sem):
    features = w.shape[0]
    chunk = features // nx
    piece = chunk // 2
    wide = nz * HID
    down, cols = pl.ds(2 * wide, wide), pl.ds(0, 2 * wide)
    spans = [pl.ds(x * chunk, chunk) for x in range(nx)]
    tail = pl.ds(features, PAD)
    moves = [(w_hbm.at[span, down], w.at[span, down]) for span in spans]
    moves += [(ext_hbm.at[:, span], ext.at[:, span]) for span in spans]
    moves += [(rows_hbm.at[:, span], rows.at[:, span]) for span in spans]
    moves += [(w_hbm.at[span, cols], w.at[span, cols]) for span in spans]
    moves += [(ext_hbm.at[:, tail], ext.at[:, tail]), (gu_hbm, gu_ref)]
    loads = [pltpu.make_async_copy(source, target, in_sem.at[n]) for n, (source, target) in enumerate(moves)]
    load_extra, load_gu = loads[4 * nx :]
    for x in range(nx):
        loads[x].start()
        loads[nx + x].start()
    load_extra.start()
    load_gu.start()
    for copy in loads[2 * nx : 4 * nx]:
        copy.start()
    down_grad = None
    for x in range(nx):
        loads[x].wait()
        loads[nx + x].wait()
        span = slice(x * chunk, (x + 1) * chunk)
        term = dot(ext[:, span], w[span, 2 * wide :], ((1,), (0,)))
        down_grad = term if x == 0 else down_grad + term
    load_extra.wait()
    extra = ext[:, features:].astype(F32)
    prob = extra[:, 0:1] + extra[:, 1:2]
    load_gu.wait()
    gate_pre, up_pre = gu_ref[:, :wide], gu_ref[:, wide:]
    sig = jax.nn.sigmoid(gate_pre)
    act = gate_pre * sig
    hidden = (act * up_pre).astype(BF16)
    scores = jnp.sum(hidden.astype(F32) * down_grad, axis=1, keepdims=True)
    hidden_grad = prob * down_grad
    gate_grad = (hidden_grad * up_pre * sig * (1.0 + gate_pre * (1.0 - sig))).astype(BF16)
    up_grad = (hidden_grad * act).astype(BF16)
    gu_grad = jnp.concatenate([gate_grad, up_grad], axis=1)
    stores = []
    for x in range(nx):
        loads[2 * nx + x].wait()
        span = slice(x * chunk, (x + 1) * chunk)
        terms[span, : 2 * wide] = dot(rows[:, span], gu_grad, ((0,), (0,))).astype(BF16)
        scaled = (prob * ext[:, span].astype(F32)).astype(BF16)
        terms[span, 2 * wide :] = dot(scaled, hidden, ((0,), (0,))).astype(BF16)
        for m, i, row, col in pieces(nz, nx, x, features):
            copy = pltpu.make_async_copy(
                terms.at[pl.ds(row, piece), pl.ds(col, HID)],
                terms_hbm.at[pl.ds(i * piece, piece), :],
                terms_sem.at[i],
            )
            copy.start()
            stores.append(copy)
    lane = lax.broadcasted_iota(jnp.int32, (scores.shape[0], PAD), 1)
    high = scores.astype(BF16).astype(F32)
    low = scores - high
    part[:, features:] = jnp.where(lane == 0, high, jnp.where(lane == 1, low, 0.0)).astype(BF16)
    for x in range(nx):
        loads[3 * nx + x].wait()
        span = slice(x * chunk, (x + 1) * chunk)
        part[:, span] = dot(gu_grad, w[span, : 2 * wide], ((1,), (1,))).astype(BF16)
        if x == nx - 1:
            span = slice(x * chunk, features + PAD)
        copy = pltpu.make_async_copy(part.at[:, span], part_hbm.at[:, span], part_sem.at[x])
        copy.start()
        stores.append(copy)
    for copy in stores:
        copy.wait()


ANYWHERE = pl.BlockSpec(memory_space=pl.ANY)
SCALAR = pl.BlockSpec(memory_space=pltpu.SMEM)
INSIDE = pl.BlockSpec(memory_space=pltpu.VMEM)


def pre_math(y, tok, w, nrows, nz, nx):
    features = tok[0].shape[1]
    wide = nz * HID
    return pl.pallas_call(
        functools.partial(pre_kernel, nz, nx, nrows // tok[0].shape[0]),
        name="pre_math",
        out_shape=(
            jax.ShapeDtypeStruct((nrows, features), BF16),
            jax.ShapeDtypeStruct((features, KINDS * wide), BF16),
            jax.ShapeDtypeStruct((nrows, 2 * wide), F32),
        ),
        in_specs=[SCALAR] + [INSIDE] * len(tok) + [ANYWHERE],
        out_specs=(INSIDE,) * 3,
        scratch_shapes=[pltpu.SemaphoreType.DMA((nz * nx * 2 * KINDS,))],
        compiler_params=pltpu.CompilerParams(vmem_limit_bytes=PRE_GRANT),
        cost_estimate=pl.CostEstimate(
            flops=4 * nrows * features * wide,
            transcendentals=0,
            bytes_accessed=2 * features * (KINDS * wide + nrows),
        ),
    )(y, *tok, w)


def expert_math(rows, ext, w, gu, held, nz, nx):
    count, features = rows.shape
    wide = nz * HID
    copies = nz * nx * 2 * KINDS
    return pl.pallas_call(
        functools.partial(expert_kernel, nz, nx),
        name="expert_math",
        out_shape=(
            pltpu.HBM((held, HID), BF16),
            jax.ShapeDtypeStruct((count, features + PAD), BF16),
        ),
        in_specs=[ANYWHERE] * 4,
        out_specs=(ANYWHERE, ANYWHERE),
        scratch_shapes=[
            pltpu.VMEM((count, features), BF16),
            pltpu.VMEM((count, features + PAD), BF16),
            pltpu.VMEM((features, KINDS * wide), BF16),
            pltpu.VMEM((count, 2 * wide), F32),
            pltpu.VMEM((features, KINDS * wide), BF16),
            pltpu.VMEM((count, features + PAD), BF16),
            pltpu.SemaphoreType.DMA((2 + 4 * nx,)),
            pltpu.SemaphoreType.DMA((copies,)),
            pltpu.SemaphoreType.DMA((nx,)),
        ],
        compiler_params=pltpu.CompilerParams(vmem_limit_bytes=EXPERT_GRANT),
        cost_estimate=pl.CostEstimate(
            flops=12 * count * features * wide,
            transcendentals=count * wide,
            bytes_accessed=2 * features * (KINDS * wide + 2 * count),
        ),
    )(rows, ext, w, gu)


def layer(tokens, grad_out, routes, route_probs, gate_weight, up_weight, down_weight):
    count, features = tokens.shape
    experts, ny = lax.axis_size("e"), lax.axis_size("y")
    nz, nx = lax.axis_size("zp"), lax.axis_size("x")
    slots = experts * CAP

    stored = jnp.concatenate([gate_weight[0], up_weight[0], down_weight[0]], axis=0)
    paired = lax.ppermute(stored, "zp", SWAP)
    weights = lax.all_gather(jnp.concatenate([stored, paired], axis=0), HOLD, axis=0, tiled=True)

    ids = jnp.arange(experts, dtype=jnp.int32)
    first, second = routes[:, 0:1] == ids, routes[:, 1:2] == ids
    named = (first | second).astype(BF16)
    place = jnp.arange(count)
    before = (place[:, None] > place[None, :]).astype(BF16)
    rank = dot(before, named, ((1,), (0,))).T
    taken = (named.T[:, None, :] > 0) & (rank[:, None, :] == jnp.arange(CAP, dtype=F32)[None, :, None])
    prob = jnp.where(first, route_probs[:, 0:1], 0.0) + jnp.where(second, route_probs[:, 1:2], 0.0)
    slot_prob = jnp.sum(jnp.where(taken, prob.T[:, None, :], 0.0), axis=2).reshape(slots)
    select = taken.astype(BF16).reshape(slots, count)
    send_tok = dot(select, tokens, ((1,), (0,))).astype(BF16)
    send_grd = dot(select, grad_out, ((1,), (0,))).astype(BF16)
    send_grd = jnp.concatenate([send_grd, columns(slot_prob)], axis=1)

    own = swapped(send_tok, "e")
    own, send_grd = lax.optimization_barrier((own, send_grd))
    up, down = [(i, (i + 1) % ny) for i in range(ny)], [(i, (i - 1) % ny) for i in range(ny)]
    half = slots // 2
    left, right = lax.ppermute(own, "y", up), lax.ppermute(own, "y", down)
    halves = left[:half], right[half:]
    far = lax.ppermute(halves[0], "y", up), lax.ppermute(halves[1], "y", down)
    came_grd = swapped(send_grd, "e")
    rows_ext = shared(came_grd, "y")

    y = lax.axis_index("y").astype(jnp.int32).reshape(1)
    rows, blocks, gate_up = pre_math(y, (own, left, right) + far, weights, ny * slots, nz, nx)
    terms, part = expert_math(rows, rows_ext, blocks, gate_up, weights.shape[0], nz, nx)
    back = swapped(part, "y")
    sums = lax.psum_scatter(terms, HOLD, scatter_dimension=0, tiled=True)
    kept, given = jnp.split(sums, 2, axis=0)
    given = lax.ppermute(given, "zp", SWAP)
    kept, given = kept.reshape(KINDS, 1, -1, HID), given.reshape(KINDS, 1, -1, HID)
    grads = [(kept[m].astype(F32) + given[m].astype(F32)).astype(BF16) for m in range(KINDS)]

    back = jnp.sum(back.astype(F32).reshape(ny, slots, -1), axis=0)
    score = back[:, features : features + 1] + back[:, features + 1 : features + 2]
    high = lax.reduce_precision(score, 8, 7)
    lane = lax.broadcasted_iota(jnp.int32, back.shape, 1)
    back = jnp.where(lane == features, high, jnp.where(lane == features + 1, score - high, back)).astype(BF16)
    back = swapped(back, "e")
    grad_tokens = dot(select, back[:, :features], ((0,), (0,))).astype(BF16)
    score = joined(back[:, features : features + 2]).reshape(experts, CAP, 1)
    score = jnp.sum(jnp.where(taken, score, 0.0), axis=1).T
    grad_probs = jnp.stack(
        [jnp.sum(jnp.where(first, score, 0.0), axis=1), jnp.sum(jnp.where(second, score, 0.0), axis=1)], axis=1
    )
    return (grad_tokens, grad_probs, grads[0], grads[1], grads[2])


def solution(mesh):
    fine = Mesh(mesh.devices.reshape(mesh.shape["ep"] // GROUP, 2, GROUP // 2, -1, 2), AXES)
    rows, stored = P(AXES, None), P(AXES[:3], AXES[3:], None)
    return jax.shard_map(
        layer,
        mesh=fine,
        in_specs=(rows, rows, rows, rows, stored, stored, stored),
        out_specs=(rows, rows, stored, stored, stored),
        check_vma=False,
    )
```
